512 devices in a mesh: seq: 64 (over y, x, z_lo), head: 8 (over z_hi, core).
Axes of the slice: x: 4, y: 8, z: 8 (z_hi: 4, z_lo: 2; z = z_hi * 2 + z_lo), core: 2. Of those that a mesh axis runs over, the one named last changes fastest.
Arguments:
- layer_input: bfloat16 [32768, 5376], P('seq', 'head'), may hold values from -6 to 6
- omega_in: bfloat16 [5376, 128], P('head'), may hold values from -0.00390625 to 0.00390625
- upstream: bfloat16 [32768, 5376], P('seq', 'head'), may hold values from -6 to 6
- omega_out: bfloat16 [5376, 128], P('head'), may hold values from -0.00390625 to 0.00390625
- q_raw: bfloat16 [32768, 4096], P('seq', 'head'), may hold values from -6 to 6
- k_raw: bfloat16 [32768, 2048], P('seq', 'head'), may hold values from -6 to 6
- values: bfloat16 [32768, 2048], P('seq', 'head'), may hold values from -6 to 6
- d_out: bfloat16 [32768, 4096], P('seq', 'head'), may hold values from -16 to 16
- q_gain: float32 [128], replicated, may hold values from 0.1 to 1.9
- k_gain: float32 [128], replicated, may hold values from 0.1 to 1.9
Outputs:
- query_grad: bfloat16 [32768, 4096], P('seq', 'head')
- key_grad: bfloat16 [32768, 2048], P('seq', 'head')
- value_grad: bfloat16 [32768, 2048], P('seq', 'head')
- sketch_q: float32 [128, 4096], P('seq', 'head')
- sketch_k: float32 [128, 2048], P('seq', 'head')
- sketch_v: float32 [128, 2048], P('seq', 'head')
- sketch_o: float32 [128, 4096], P('seq', 'head')
The draws below stay inside these ranges and needn't reach their ends.
All inputs are finite; a program needn't handle non-finite values.
Results may differ from the reference program's by a relative error of at most 0.013.
Values may be sent and summed in bfloat16 or wider, within the bound.
No kernel may reach another device: no remote copies, remote signals or barrier semaphores. Data moves between devices by JAX's collectives and lax.ppermute only.
A program may use at most 64 MiB of HBM per device.

```python
import jax
import jax.numpy as jnp
from jax import lax

D = 5376
QH = 32
KH = 16
HD = 128
WINDOW = 1024
RANK = 128
TOK_DEV = 512
TOKENS = 32768
HALO_DEV = 2


def steps_of(rng, dims, pieces, smallest, high):
    level = 1.0
    for axis_at, parts in pieces:
        draws = jax.random.uniform(jax.random.fold_in(jax.random.fold_in(rng, 6), axis_at), (parts,), jnp.float32, smallest / len(pieces), high / len(pieces))
        level = level * jnp.repeat(jnp.exp(draws), dims[axis_at] // parts).reshape((-1,) + (1,) * (len(dims) - 1 - axis_at))
    return level


def gaussian(own_key, extent, spread, most, pieces=(), kind=jnp.bfloat16):
    drawn = jax.random.normal(own_key, extent, jnp.float32) * spread
    if len(pieces) > 0:
        drawn = steps_of(own_key, extent, pieces, -0.22, 0.18) * drawn
    return jnp.clip(drawn, min=-most, max=most).astype(kind)


def setup_inputs(seed: int = 0) -> dict:
    key_of = jax.random.split(jax.random.key(seed), 11)
    return {
        "layer_input": gaussian(key_of[0], (TOKENS, D), 1.0, 6.0, ((0, 64), (1, 8))),
        "omega_in": gaussian(key_of[1], (D, RANK), (D * TOKENS // 64) ** -0.5, 0.00390625, ((0, 8),)),
        "upstream": gaussian(key_of[2], (TOKENS, D), 1.0, 6.0, ((0, 64), (1, 8))),
        "omega_out": gaussian(key_of[3], (D, RANK), (D * TOKENS // 64) ** -0.5, 0.00390625, ((0, 8),)),
        "q_raw": gaussian(key_of[4], (TOKENS, QH * HD), 1.0, 6.0, ((0, 64), (1, 8))),
        "k_raw": gaussian(key_of[5], (TOKENS, KH * HD), 1.0, 6.0, ((0, 64), (1, 8))),
        "values": gaussian(key_of[6], (TOKENS, KH * HD), 1.0, 6.0, ((0, 64), (1, 8))),
        "d_out": gaussian(key_of[7], (TOKENS, QH * HD), 4.0, 16.0, ((0, 64), (1, 8))),
        "q_gain": jnp.clip(1.0 + 0.18 * jax.random.normal(key_of[8], (HD,), jnp.float32), 0.1, 1.9),
        "k_gain": jnp.clip(1.0 + 0.18 * jax.random.normal(key_of[9], (HD,), jnp.float32), 0.1, 1.9),
    }


score_scale = 168.0 ** (-0.5)
epsilon = 1e-06
rope_base = 10000.0

def prepare(raw_input, gain, positions):
    mean_square = lax.optimization_barrier(jnp.mean(raw_input * raw_input, axis=-1, keepdims=True))
    normed = raw_input * lax.rsqrt(mean_square + epsilon) * gain
    half_dim = raw_input.shape[-1] // 2
    inverse_freq = rope_base ** (-(jnp.arange(half_dim, dtype=jnp.float32) * 2.0 / raw_input.shape[-1]))
    angles = positions.astype(jnp.float32)[:, None] * inverse_freq[None, :]
    cos_table = jnp.cos(angles)[:, None, :]
    sin_table = jnp.sin(angles)[:, None, :]
    lower_half = normed[..., :half_dim]
    upper_half = normed[..., half_dim:]
    return jnp.concatenate([lower_half * cos_table - upper_half * sin_table, upper_half * cos_table + lower_half * sin_table], axis=-1)

def head_core(query_rows, key_rows, value_rows, grad_rows, allowed):
    scores = score_scale * jnp.dot(query_rows, key_rows.T, preferred_element_type=jnp.float32)
    exp_scores = jnp.where(allowed, jnp.exp(scores), 0.0)
    probs = exp_scores / lax.optimization_barrier(jnp.sum(exp_scores, axis=-1, keepdims=True))
    probs_low = probs.astype(jnp.bfloat16)
    attn_rows = jnp.dot(probs_low, value_rows, preferred_element_type=jnp.float32).astype(jnp.bfloat16)
    grad_probs = jnp.dot(grad_rows, value_rows.T, preferred_element_type=jnp.float32)
    row_delta = lax.optimization_barrier(jnp.sum(probs * grad_probs, axis=-1, keepdims=True))
    grad_low = (probs * (grad_probs - row_delta)).astype(jnp.bfloat16)
    query_grad = score_scale * jnp.dot(grad_low, key_rows, preferred_element_type=jnp.float32)
    key_grad = score_scale * jnp.dot(grad_low.T, query_rows, preferred_element_type=jnp.float32)
    value_grad = jnp.dot(probs_low.T, grad_rows, preferred_element_type=jnp.float32)
    return (attn_rows, query_grad, key_grad, value_grad)

def reference(layer_input, omega_in, upstream, omega_out, q_raw, k_raw, values, d_out, q_gain, k_gain):
    tokens = q_raw.shape[0]
    group_size = QH // KH
    ext_rows = HALO_DEV * TOK_DEV
    span_rows = ext_rows + TOK_DEV
    positions = jnp.arange(tokens, dtype=jnp.int32)
    query_f = q_raw.astype(jnp.float32).reshape(tokens, QH, HD)
    key_f = k_raw.astype(jnp.float32).reshape(tokens, KH, HD)
    query_full, query_back = jax.vjp(lambda raw_input: prepare(raw_input, q_gain, positions), query_f)
    key_full, key_back = jax.vjp(lambda raw_input: prepare(raw_input, k_gain, positions), key_f)
    query_prep = query_full.astype(jnp.bfloat16)
    key_prep = key_full.astype(jnp.bfloat16)
    key_pad = jnp.concatenate([jnp.zeros((ext_rows, KH, HD), jnp.bfloat16), key_prep], axis=0)
    value_pad = jnp.concatenate([jnp.zeros((ext_rows, KH, HD), jnp.bfloat16), values.reshape(tokens, KH, HD)], axis=0)
    grad_all = d_out.reshape(tokens, QH, HD)
    row_index = jnp.arange(TOK_DEV, dtype=jnp.int32)[:, None]
    col_index = jnp.arange(span_rows, dtype=jnp.int32)[None, :]
    gap = row_index - col_index + ext_rows

    def block_step(carried, block_index):
        key_acc, value_acc = carried
        begin_row = block_index * TOK_DEV
        key_pos = begin_row - ext_rows + col_index
        allowed = (key_pos >= 0) & (gap >= 0) & (gap < WINDOW)
        query_blk = lax.dynamic_slice_in_dim(query_prep, begin_row, TOK_DEV, 0).transpose(1, 0, 2)
        grad_blk = lax.dynamic_slice_in_dim(grad_all, begin_row, TOK_DEV, 0).transpose(1, 0, 2)
        key_blk = lax.dynamic_slice_in_dim(key_pad, begin_row, span_rows, 0).transpose(1, 0, 2)
        value_blk = lax.dynamic_slice_in_dim(value_pad, begin_row, span_rows, 0).transpose(1, 0, 2)
        key_rep = jnp.repeat(key_blk, group_size, axis=0)
        value_rep = jnp.repeat(value_blk, group_size, axis=0)
        attn_blk, query_grad, key_grad, value_grad = lax.map(lambda items: head_core(items[0], items[1], items[2], items[3], allowed), (query_blk, key_rep, value_rep, grad_blk))
        key_sum = key_grad.reshape(KH, group_size, span_rows, HD).sum(axis=1).transpose(1, 0, 2)
        value_sum = value_grad.reshape(KH, group_size, span_rows, HD).sum(axis=1).transpose(1, 0, 2)
        key_acc = lax.dynamic_update_slice_in_dim(key_acc, lax.dynamic_slice_in_dim(key_acc, begin_row, span_rows, 0) + key_sum, begin_row, 0)
        value_acc = lax.dynamic_update_slice_in_dim(value_acc, lax.dynamic_slice_in_dim(value_acc, begin_row, span_rows, 0) + value_sum, begin_row, 0)
        return ((key_acc, value_acc), (attn_blk, query_grad))
    zero_acc = jnp.zeros((ext_rows + tokens, KH, HD), jnp.float32)
    (key_acc, value_acc), (attn_all, query_all) = lax.scan(block_step, (zero_acc, zero_acc), jnp.arange(tokens // TOK_DEV, dtype=jnp.int32))
    attn_out = attn_all.transpose(0, 2, 1, 3).reshape(tokens, QH * HD)
    query_grad_prep = query_all.transpose(0, 2, 1, 3).reshape(tokens, QH, HD)
    query_grad = query_back(query_grad_prep)[0].reshape(tokens, QH * HD).astype(jnp.bfloat16)
    key_grad = key_back(key_acc[ext_rows:])[0].reshape(tokens, KH * HD).astype(jnp.bfloat16)
    value_grad = value_acc[ext_rows:].reshape(tokens, KH * HD).astype(jnp.bfloat16)
    x_sketch = jnp.dot(layer_input, omega_in, preferred_element_type=jnp.float32).astype(jnp.bfloat16)
    dy_sketch = jnp.dot(upstream, omega_out, preferred_element_type=jnp.float32).astype(jnp.bfloat16)
    sketch_q = jnp.dot(x_sketch.T, query_grad, preferred_element_type=jnp.float32)
    sketch_k = jnp.dot(x_sketch.T, key_grad, preferred_element_type=jnp.float32)
    sketch_v = jnp.dot(x_sketch.T, value_grad, preferred_element_type=jnp.float32)
    sketch_o = jnp.dot(dy_sketch.T, attn_out, preferred_element_type=jnp.float32)
    return (query_grad, key_grad, value_grad, sketch_q, sketch_k, sketch_v, sketch_o)
```

```python
import jax
import jax.numpy as jnp
import numpy as np
from jax import lax
from jax.experimental import pallas as pl
from jax.experimental.pallas import tpu as pltpu
from jax.sharding import PartitionSpec as P

WINDOW = 1024
HD = 128
TOK = 512
QT = 256
KB = 256
SPAN = 1536
NBLK = 5
score_scale = 168.0 ** (-0.5)
LOG2E = 1.4426950408889634
epsilon = 1e-06
rope_base = 10000.0
F32 = jnp.float32
BF16 = jnp.bfloat16


def rope_tables(shards):
    freq = rope_base ** (-(np.arange(64, dtype=np.float64) * 2.0 / HD))
    freq = np.concatenate([freq, freq])[None, :]
    base = ((np.arange(shards + 2) - 2) * TOK).astype(np.float64)[:, None] * freq
    local = np.arange(TOK, dtype=np.float64)[:, None] * freq
    pad = (-base.shape[0]) % 8
    base = np.pad(base, ((0, pad), (0, 0)))
    tables = [np.cos(base), np.sin(base), np.cos(local), np.sin(local)]
    return [t.astype(np.float32) for t in tables]


def norm_scale(raw):
    return lax.rsqrt(jnp.mean(raw * raw, axis=-1, keepdims=True) + epsilon)


def rope_forward(normed, cos, sin_signed):
    return normed * cos + pltpu.roll(normed, 64, 1) * sin_signed


def prep_back(raw, gain, cos, sin_signed, grad):
    r = norm_scale(raw)
    d_norm = (grad * cos - pltpu.roll(grad, 64, 1) * sin_signed) * gain
    return r * d_norm - raw * ((r * r * r) * jnp.mean(raw * d_norm, axis=-1, keepdims=True))


def mm(a, b):
    return lax.dot_general(a, b, (((1,), (0,)), ((), ())), preferred_element_type=F32)


def mm_t(a, b):
    return lax.dot_general(a, b, (((1,), (1,)), ((), ())), preferred_element_type=F32)


def attention_kernel(
    shard_ref, q_ref, do_ref, k0_ref, k1_ref, k2_ref, v0_ref, v1_ref, v2_ref,
    qg_ref, kg_ref, cb_ref, sb_ref, cl_ref, sl_ref,
    qgrad_ref, attn_ref, dk_ref, dv_ref, back1_ref, back2_ref,
    kp, vx, cos, sin, e_sc, dp_sc, dkt, dvt,
):
    tile = pl.program_id(1)
    shard = shard_ref[0]

    @pl.when((pl.program_id(0) == 0) & (tile == 0))
    def _():
        lane = lax.broadcasted_iota(jnp.int32, (1, HD), 1)
        sign = jnp.where(lane < HD // 2, -1.0, 1.0)
        for part in range(3):
            cb = cb_ref[pl.ds(shard + part, 1), :]
            sb = sb_ref[pl.ds(shard + part, 1), :]
            rows = slice(part * TOK, (part + 1) * TOK)
            cos[rows, :] = cb * cl_ref[...] - sb * sl_ref[...]
            sin[rows, :] = (sb * cl_ref[...] + cb * sl_ref[...]) * sign

    @pl.when(tile == 0)
    def _():
        for part, (k_ref, v_ref) in enumerate(((k2_ref, v2_ref), (k1_ref, v1_ref), (k0_ref, v0_ref))):
            rows = slice(part * TOK, (part + 1) * TOK)
            raw = k_ref[...].astype(F32)
            normed = raw * norm_scale(raw) * kg_ref[...]
            kp[rows, :] = rope_forward(normed, cos[rows, :], sin[rows, :]).astype(BF16)
            vx[rows, :] = v_ref[...]
        dkt[...] = jnp.zeros_like(dkt)
        dvt[...] = jnp.zeros_like(dvt)

    q_rows = pl.ds(pl.multiple_of(2 * TOK + tile * QT, QT), QT)
    cos_q = cos[q_rows, :]
    sin_q = sin[q_rows, :]
    q_parts = []
    for g in range(2):
        raw = q_ref[:, g * HD : (g + 1) * HD].astype(F32)
        normed = raw * norm_scale(raw) * qg_ref[...]
        q_parts.append(rope_forward(normed, cos_q, sin_q))
    q = jnp.concatenate(q_parts, axis=0)
    d_out = jnp.concatenate([do_ref[:, :HD], do_ref[:, HD:]], axis=0)
    q_low = q.astype(BF16)
    q_t = q.T.astype(BF16)
    do_t = d_out.astype(F32).T.astype(BF16)

    rows_i = lax.broadcasted_iota(jnp.int32, (QT, KB), 0)
    cols_i = lax.broadcasted_iota(jnp.int32, (QT, KB), 1)
    lower = (cols_i <= rows_i).astype(F32)
    upper = 1.0 - lower
    lower = jnp.concatenate([lower, lower], axis=0)
    upper = jnp.concatenate([upper, upper], axis=0)

    l_acc = jnp.zeros((2 * QT, HD), F32)
    u_acc = jnp.zeros((2 * QT, HD), F32)
    for b in range(NBLK):
        at = pl.ds(pl.multiple_of(tile * QT + b * KB, KB), KB)
        cols = slice(b * KB, (b + 1) * KB)
        s = mm_t(q_low, kp[at, :])
        e = jnp.exp2(s * (score_scale * LOG2E))
        key_shard = shard - 2 + (tile * QT + b * KB) // TOK
        if b == 0:
            e = e * (upper * jnp.where(key_shard >= 0, 1.0, 0.0))
        elif b == NBLK - 1:
            e = e * lower
        else:
            e = e * jnp.where(key_shard >= 0, 1.0, 0.0)
        dp = mm_t(d_out, vx[at, :])
        ed = e * dp
        l_acc = l_acc + e[:, :HD] + e[:, HD:]
        u_acc = u_acc + ed[:, :HD] + ed[:, HD:]
        e_sc[:, cols] = e
        dp_sc[:, cols] = dp
    inv = 1.0 / jnp.sum(l_acc, axis=-1, keepdims=True)
    delta = jnp.sum(u_acc, axis=-1, keepdims=True) * inv

    out = jnp.zeros((2 * QT, HD), F32)
    dq = jnp.zeros((2 * QT, HD), F32)
    for b in range(NBLK):
        at = pl.ds(pl.multiple_of(tile * QT + b * KB, KB), KB)
        cols = slice(b * KB, (b + 1) * KB)
        p = e_sc[:, cols] * inv
        ds = (p * (dp_sc[:, cols] - delta)).astype(BF16)
        p = p.astype(BF16)
        out = out + mm(p, vx[at, :])
        dq = dq + mm(ds, kp[at, :])
        dvt[:, at] += mm(do_t, p)
        dkt[:, at] += mm(q_t, ds)
    for g in range(2):
        rows = slice(g * QT, (g + 1) * QT)
        lanes = slice(g * HD, (g + 1) * HD)
        attn_ref[:, lanes] = out[rows].astype(BF16)
        raw = q_ref[:, lanes].astype(F32)
        qgrad_ref[:, lanes] = prep_back(
            raw, qg_ref[...], cos_q, sin_q, dq[rows] * score_scale
        ).astype(BF16)

    @pl.when(tile == 1)
    def _():
        for part, k_ref in enumerate((k2_ref, k1_ref, k0_ref)):
            rows = slice(part * TOK, (part + 1) * TOK)
            raw = k_ref[...].astype(F32)
            dk = prep_back(
                raw, kg_ref[...], cos[rows, :], sin[rows, :], dkt[:, rows].T * score_scale
            )
            dv = dvt[:, rows].T
            if part == 2:
                dk_ref[...] = dk
                dv_ref[...] = dv
            else:
                back = back2_ref if part == 0 else back1_ref
                back[0, 0] = dk.astype(BF16)
                back[0, 1] = dv.astype(BF16)


def attention(shard, q_raw, d_out, k_raw, values, kv1, kv2, q_gain, k_gain, tables):
    whole = lambda a: pl.BlockSpec(a.shape, lambda h, t: (0,) * a.ndim)
    tile_spec = pl.BlockSpec((QT, 2 * HD), lambda h, t: (t, h))
    k_spec = pl.BlockSpec((TOK, HD), lambda h, t: (0, h))
    v_spec = pl.BlockSpec((TOK, HD), lambda h, t: (0, 2 + h))
    back_spec = pl.BlockSpec((1, 2, TOK, HD), lambda h, t: (h, 0, 0, 0))
    back_shape = jax.ShapeDtypeStruct((2, 2, TOK, HD), BF16)
    gains = [q_gain[None, :], k_gain[None, :]]
    return pl.pallas_call(
        attention_kernel,
        grid=(2, 2),
        in_specs=[
            pl.BlockSpec(memory_space=pltpu.SMEM),
            tile_spec, tile_spec,
            k_spec, k_spec, k_spec, k_spec, v_spec, v_spec,
        ] + [whole(a) for a in gains + tables],
        out_specs=[tile_spec, tile_spec, k_spec, k_spec, back_spec, back_spec],
        out_shape=[
            jax.ShapeDtypeStruct((TOK, 4 * HD), BF16),
            jax.ShapeDtypeStruct((TOK, 4 * HD), BF16),
            jax.ShapeDtypeStruct((TOK, 2 * HD), F32),
            jax.ShapeDtypeStruct((TOK, 2 * HD), F32),
            back_shape, back_shape,
        ],
        scratch_shapes=[
            pltpu.VMEM((SPAN, HD), BF16),
            pltpu.VMEM((SPAN, HD), BF16),
            pltpu.VMEM((SPAN, HD), F32),
            pltpu.VMEM((SPAN, HD), F32),
            pltpu.VMEM((2 * QT, NBLK * KB), F32),
            pltpu.VMEM((2 * QT, NBLK * KB), F32),
            pltpu.VMEM((HD, SPAN), F32),
            pltpu.VMEM((HD, SPAN), F32),
        ],
        compiler_params=pltpu.CompilerParams(vmem_limit_bytes=40 << 20),
        cost_estimate=pl.CostEstimate(
            flops=6 * 4 * 2 * TOK * SPAN * HD, bytes_accessed=6 << 20, transcendentals=4 * TOK * SPAN
        ),
    )(shard, q_raw, d_out, k_raw, kv1, kv2, values, kv1, kv2, *gains, *tables)


def sketch_kernel(x0_ref, x1_ref, x2_ref, y_ref, qgrad_ref, attn_ref, dk_ref, dv_ref, b1_ref, b2_ref, out_ref):
    def tokens(a, b):
        return lax.dot_general(a, b, (((0,), (0,)), ((), ())), preferred_element_type=F32)

    x0, x1, x2 = x0_ref[...], x1_ref[...], x2_ref[...]
    out_ref[:, 0 : 4 * HD] = tokens(x0, qgrad_ref[...]).astype(BF16)
    out_ref[:, 8 * HD : 12 * HD] = tokens(y_ref[...], attn_ref[...]).astype(BF16)
    for kind, own_ref in enumerate((dk_ref, dv_ref)):
        for h in range(2):
            total = tokens(x0, own_ref[:, h * HD : (h + 1) * HD].astype(BF16))
            total += tokens(x1, b1_ref[h, kind])
            total += tokens(x2, b2_ref[h, kind])
            at = (4 + 2 * kind + h) * HD
            out_ref[:, at : at + HD] = total.astype(BF16)


def sketch(*args):
    return pl.pallas_call(
        sketch_kernel,
        out_shape=jax.ShapeDtypeStruct((HD, 12 * HD), BF16),
        compiler_params=pltpu.CompilerParams(vmem_limit_bytes=24 << 20),
        cost_estimate=pl.CostEstimate(
            flops=2 * TOK * HD * 16 * HD, bytes_accessed=5 << 20, transcendentals=0
        ),
    )(*args)


def shift(x, by):
    count = lax.axis_size("seq")
    pairs = [(i, i + by) for i in range(count) if 0 <= i + by < count]
    return lax.ppermute(x, "seq", pairs)


def swap(x, bit):
    count = lax.axis_size("head")
    return lax.ppermute(x, "head", [(i, i ^ bit) for i in range(count)])


def sum_over_head(partial_x, partial_y):
    first = lax.axis_index("head") % 2 == 0
    got = swap(jnp.where(first, partial_y, partial_x).astype(BF16), 1)
    total = jnp.where(first, partial_x, partial_y) + got.astype(F32)
    for bit in (2, 4):
        total = total + swap(total.astype(BF16), bit).astype(F32)
    mine = total.astype(BF16)
    other = swap(mine, 1)
    return jnp.where(first, mine, other), jnp.where(first, other, mine)


def per_device(
    layer_input, omega_in, upstream, omega_out, q_raw, k_raw, values, d_out, q_gain, k_gain
):
    kv = jnp.concatenate([k_raw, values], axis=1)
    kv2 = shift(kv, 2)
    kv1 = shift(kv, 1)
    partial_x = jnp.dot(layer_input, omega_in, preferred_element_type=F32)
    partial_y = jnp.dot(upstream, omega_out, preferred_element_type=F32)
    x0, y0 = sum_over_head(partial_x, partial_y)
    x1 = shift(x0, 1)
    x2 = shift(x0, 2)
    shard = lax.axis_index("seq").astype(jnp.int32)[None]
    tables = [jnp.asarray(t) for t in rope_tables(lax.axis_size("seq"))]
    query_grad, attn_out, dk, dv, back1, back2 = attention(
        shard, q_raw, d_out, k_raw, values, kv1, kv2, q_gain, k_gain, tables
    )
    got2 = shift(back2, -2)
    got1 = shift(back1, -1)
    sketches = sketch(x0, x1, x2, y0, query_grad, attn_out, dk, dv, back1, back2)
    shards = lax.axis_size("seq")
    pieces = lax.all_to_all(sketches.reshape(shards, HD // shards, 12 * HD), "seq", 0, 0, tiled=True)
    total = jnp.sum(pieces.astype(F32), axis=0)

    def finish(own, kind):
        far = (got1[:, kind].astype(F32) + got2[:, kind].astype(F32)).transpose(1, 0, 2)
        return (own + far.reshape(own.shape)).astype(BF16)

    q_cols, kv_cols = 4 * HD, 2 * HD
    return (
        query_grad,
        finish(dk, 0),
        finish(dv, 1),
        total[:, :q_cols],
        total[:, q_cols : q_cols + kv_cols],
        total[:, q_cols + kv_cols : q_cols + 2 * kv_cols],
        total[:, q_cols + 2 * kv_cols :],
    )


def solution(mesh):
    split = P("seq", "head")
    in_specs = (split, P("head", None), split, P("head", None), split, split, split, split, P(), P())
    return jax.shard_map(
        per_device, mesh=mesh, in_specs=in_specs, out_specs=(split,) * 7, check_vma=False
    )
```

```python
import jax
import jax.numpy as jnp
import numpy as np
from jax import lax
from jax.experimental import pallas as pl
from jax.experimental.pallas import tpu as pltpu
from jax.sharding import PartitionSpec as P

WINDOW = 1024
HD = 128
TOK = 512
QT = 256
KB = 256
ATTN_VMEM = 60 << 20
SPAN = 1536
NBLK = 5
score_scale = 168.0 ** (-0.5)
LOG2E = 1.4426950408889634
epsilon = 1e-06
rope_base = 10000.0
F32 = jnp.float32
BF16 = jnp.bfloat16


def rope_tables(shards):
    freq = rope_base ** (-(np.arange(64, dtype=np.float64) * 2.0 / HD))
    freq = np.concatenate([freq, freq])[None, :]
    base = ((np.arange(shards + 2) - 2) * TOK).astype(np.float64)[:, None] * freq
    local = np.arange(TOK, dtype=np.float64)[:, None] * freq
    pad = (-base.shape[0]) % 8
    base = np.pad(base, ((0, pad), (0, 0)))
    tables = [np.cos(base), np.sin(base), np.cos(local), np.sin(local)]
    return [t.astype(np.float32) for t in tables]


def norm_scale(raw):
    return lax.rsqrt(jnp.mean(raw * raw, axis=-1, keepdims=True) + epsilon)


def rope_forward(normed, cos, sin_signed):
    return normed * cos + pltpu.roll(normed, 64, 1) * sin_signed


def prep_back(raw, gain, cos, sin_signed, grad):
    r = norm_scale(raw)
    d_norm = (grad * cos - pltpu.roll(grad, 64, 1) * sin_signed) * gain
    return r * d_norm - raw * ((r * r * r) * jnp.mean(raw * d_norm, axis=-1, keepdims=True))


def mm(a, b):
    return lax.dot_general(a, b, (((1,), (0,)), ((), ())), preferred_element_type=F32)


def mm_t(a, b):
    return lax.dot_general(a, b, (((1,), (1,)), ((), ())), preferred_element_type=F32)


def attention_kernel(
    shard_ref, q_ref, do_ref, k0_ref, v0_ref, kv1_ref, kv2_ref,
    x0_ref, x1_ref, x2_ref, y_ref, qg_ref, kg_ref, cb_ref, sb_ref, cl_ref, sl_ref,
    qgrad_ref, own_ref, back1_ref, back2_ref, sk_ref,
    kp, vx, cos, sin, e_sc, dp_sc, dkt, dvt, xt, yt, skq, sko,
):
    tile = pl.program_id(1)
    shard = shard_ref[0]
    k_lanes = pl.ds(pl.multiple_of(pl.program_id(0) * HD, HD), HD)
    v_lanes = pl.ds(pl.multiple_of(pl.program_id(0) * HD + 2 * HD, HD), HD)
    k_parts = (kv2_ref.at[:, k_lanes], kv1_ref.at[:, k_lanes], k0_ref)
    v_parts = (kv2_ref.at[:, v_lanes], kv1_ref.at[:, v_lanes], v0_ref)

    @pl.when((pl.program_id(0) == 0) & (tile == 0))
    def _():
        lane = lax.broadcasted_iota(jnp.int32, (1, HD), 1)
        sign = jnp.where(lane < HD // 2, -1.0, 1.0)
        for part in range(3):
            cb = cb_ref[pl.ds(shard + part, 1), :]
            sb = sb_ref[pl.ds(shard + part, 1), :]
            rows = slice(part * TOK, (part + 1) * TOK)
            cos[rows, :] = cb * cl_ref[...] - sb * sl_ref[...]
            sin[rows, :] = (sb * cl_ref[...] + cb * sl_ref[...]) * sign

        for part, x_ref in enumerate((x2_ref, x1_ref, x0_ref)):
            xt[:, part * TOK : (part + 1) * TOK] = x_ref[...].astype(F32).T.astype(BF16)
        yt[...] = y_ref[...].astype(F32).T.astype(BF16)

    @pl.when(tile == 0)
    def _():
        skq[...] = jnp.zeros_like(skq)
        sko[...] = jnp.zeros_like(sko)
        for part, (k_ref, v_ref) in enumerate(zip(k_parts, v_parts)):
            rows = slice(part * TOK, (part + 1) * TOK)
            raw = k_ref[...].astype(F32)
            normed = raw * norm_scale(raw) * kg_ref[...]
            kp[rows, :] = rope_forward(normed, cos[rows, :], sin[rows, :]).astype(BF16)
            vx[rows, :] = v_ref[...]
        dkt[...] = jnp.zeros_like(dkt)
        dvt[...] = jnp.zeros_like(dvt)

    q_rows = pl.ds(pl.multiple_of(2 * TOK + tile * QT, QT), QT)
    cos_q = cos[q_rows, :]
    sin_q = sin[q_rows, :]
    q_parts = []
    for g in range(2):
        raw = q_ref[:, g * HD : (g + 1) * HD].astype(F32)
        normed = raw * norm_scale(raw) * qg_ref[...]
        q_parts.append(rope_forward(normed, cos_q, sin_q))
    q = jnp.concatenate(q_parts, axis=0)
    d_out = jnp.concatenate([do_ref[:, :HD], do_ref[:, HD:]], axis=0)
    q_low = q.astype(BF16)
    q_t = q.T.astype(BF16)
    do_t = d_out.astype(F32).T.astype(BF16)

    rows_i = lax.broadcasted_iota(jnp.int32, (QT, KB), 0)
    cols_i = lax.broadcasted_iota(jnp.int32, (QT, KB), 1)
    lower = (cols_i <= rows_i).astype(F32)
    upper = 1.0 - lower
    lower = jnp.concatenate([lower, lower], axis=0)
    upper = jnp.concatenate([upper, upper], axis=0)

    l_acc = jnp.zeros((2 * QT, HD), F32)
    u_acc = jnp.zeros((2 * QT, HD), F32)
    for b in range(NBLK):
        at = pl.ds(pl.multiple_of(tile * QT + b * KB, KB), KB)
        cols = slice(b * KB, (b + 1) * KB)
        s = mm_t(q_low, kp[at, :])
        e = jnp.exp2(s * (score_scale * LOG2E))
        key_shard = shard - 2 + (tile * QT + b * KB) // TOK
        if b == 0:
            e = e * (upper * jnp.where(key_shard >= 0, 1.0, 0.0))
        elif b == NBLK - 1:
            e = e * lower
        else:
            e = e * jnp.where(key_shard >= 0, 1.0, 0.0)
        dp = mm_t(d_out, vx[at, :])
        ed = e * dp
        l_acc = l_acc + e[:, :HD] + e[:, HD:]
        u_acc = u_acc + ed[:, :HD] + ed[:, HD:]
        e_sc[:, cols] = e
        dp_sc[:, cols] = dp
    inv = 1.0 / jnp.sum(l_acc, axis=-1, keepdims=True)
    delta = jnp.sum(u_acc, axis=-1, keepdims=True) * inv

    out = jnp.zeros((2 * QT, HD), F32)
    dq = jnp.zeros((2 * QT, HD), F32)
    for b in range(NBLK):
        at = pl.ds(pl.multiple_of(tile * QT + b * KB, KB), KB)
        cols = slice(b * KB, (b + 1) * KB)
        p = e_sc[:, cols] * inv
        ds = (p * (dp_sc[:, cols] - delta)).astype(BF16)
        p = p.astype(BF16)
        out = out + mm(p, vx[at, :])
        dq = dq + mm(ds, kp[at, :])
        dvt[:, at] += mm(do_t, p)
        dkt[:, at] += mm(q_t, ds)
    x_tile = xt[:, q_rows]
    y_tile = yt[:, pl.ds(pl.multiple_of(tile * QT, QT), QT)]
    for g in range(2):
        rows = slice(g * QT, (g + 1) * QT)
        lanes = slice(g * HD, (g + 1) * HD)
        raw = q_ref[:, lanes].astype(F32)
        q_grad = prep_back(raw, qg_ref[...], cos_q, sin_q, dq[rows] * score_scale).astype(BF16)
        qgrad_ref[:, lanes] = q_grad
        skq[:, lanes] += mm(x_tile, q_grad)
        sko[:, lanes] += mm(y_tile, out[rows].astype(BF16))

    @pl.when(tile == 1)
    def _():
        sk_k = jnp.zeros((HD, HD), F32)
        sk_v = jnp.zeros((HD, HD), F32)
        for part, k_ref in enumerate(k_parts):
            rows = slice(part * TOK, (part + 1) * TOK)
            raw = k_ref[...].astype(F32)
            dk = prep_back(
                raw, kg_ref[...], cos[rows, :], sin[rows, :], dkt[:, rows].T * score_scale
            )
            dv = dvt[:, rows].T
            sk_k = sk_k + mm(xt[:, rows], dk.astype(BF16))
            sk_v = sk_v + mm(xt[:, rows], dv.astype(BF16))
            target = (back2_ref, back1_ref, own_ref)[part]
            target[:, k_lanes] = dk.astype(target.dtype)
            target[:, v_lanes] = dv.astype(target.dtype)
        head = pl.program_id(0)
        sk_ref[:, pl.ds(pl.multiple_of(head * 2 * HD, 2 * HD), 2 * HD)] = skq[...].astype(BF16)
        sk_ref[:, pl.ds(pl.multiple_of(head * HD + 4 * HD, HD), HD)] = sk_k.astype(BF16)
        sk_ref[:, pl.ds(pl.multiple_of(head * HD + 6 * HD, HD), HD)] = sk_v.astype(BF16)
        sk_ref[:, pl.ds(pl.multiple_of(head * 2 * HD + 8 * HD, 2 * HD), 2 * HD)] = sko[...].astype(BF16)


def attention(shard, q_raw, d_out, k_raw, values, kv1, kv2, sketches, q_gain, k_gain, tables):
    whole = lambda a: pl.BlockSpec(a.shape, lambda h, t: (0,) * a.ndim)
    tile_spec = pl.BlockSpec((QT, 2 * HD), lambda h, t: (t, h))
    k_spec = pl.BlockSpec((TOK, HD), lambda h, t: (0, h))
    consts = [kv1, kv2, *sketches, q_gain[None, :], k_gain[None, :]] + tables
    q_shape = jax.ShapeDtypeStruct((TOK, 4 * HD), BF16)
    kv_shape = jax.ShapeDtypeStruct((TOK, 4 * HD), BF16)
    own_shape = jax.ShapeDtypeStruct((TOK, 4 * HD), F32)
    sk_shape = jax.ShapeDtypeStruct((HD, 12 * HD), BF16)
    return pl.pallas_call(
        attention_kernel,
        grid=(2, 2),
        in_specs=[pl.BlockSpec(memory_space=pltpu.SMEM), tile_spec, tile_spec, k_spec, k_spec]
        + [whole(a) for a in consts],
        out_specs=[tile_spec, whole(own_shape), whole(kv_shape), whole(kv_shape), whole(sk_shape)],
        out_shape=[q_shape, own_shape, kv_shape, kv_shape, sk_shape],
        scratch_shapes=[
            pltpu.VMEM((SPAN, HD), BF16),
            pltpu.VMEM((SPAN, HD), BF16),
            pltpu.VMEM((SPAN, HD), F32),
            pltpu.VMEM((SPAN, HD), F32),
            pltpu.VMEM((2 * QT, NBLK * KB), F32),
            pltpu.VMEM((2 * QT, NBLK * KB), F32),
            pltpu.VMEM((HD, SPAN), F32),
            pltpu.VMEM((HD, SPAN), F32),
            pltpu.VMEM((HD, SPAN), BF16),
            pltpu.VMEM((HD, TOK), BF16),
            pltpu.VMEM((HD, 2 * HD), F32),
            pltpu.VMEM((HD, 2 * HD), F32),
        ],
        compiler_params=pltpu.CompilerParams(vmem_limit_bytes=ATTN_VMEM),
        cost_estimate=pl.CostEstimate(
            flops=6 * 4 * 2 * TOK * SPAN * HD, bytes_accessed=6 << 20, transcendentals=4 * TOK * SPAN
        ),
    )(shard, q_raw, d_out, k_raw, values, *consts)


def shift(x, by):
    count = lax.axis_size("seq")
    pairs = [(i, i + by) for i in range(count) if 0 <= i + by < count]
    return lax.ppermute(x, "seq", pairs)


def swap(x, bit):
    count = lax.axis_size("head")
    return lax.ppermute(x, "head", [(i, i ^ bit) for i in range(count)])


def sum_over_head(partial_x, partial_y):
    first = lax.axis_index("head") % 2 == 0
    got = swap(jnp.where(first, partial_y, partial_x).astype(BF16), 1)
    total = jnp.where(first, partial_x, partial_y) + got.astype(F32)
    for bit in (2, 4):
        total = total + swap(total.astype(BF16), bit).astype(F32)
    mine = total.astype(BF16)
    other = swap(mine, 1)
    return jnp.where(first, mine, other), jnp.where(first, other, mine)


def per_device(
    layer_input, omega_in, upstream, omega_out, q_raw, k_raw, values, d_out, q_gain, k_gain
):
    kv = jnp.concatenate([k_raw, values], axis=1)
    kv, layer_input, upstream = lax.optimization_barrier((kv, layer_input, upstream))
    kv2 = shift(kv, 2)
    kv1 = shift(kv, 1)
    partial_x = jnp.dot(layer_input, omega_in, preferred_element_type=F32)
    partial_y = jnp.dot(upstream, omega_out, preferred_element_type=F32)
    x0, y0 = lax.fori_loop(
        0,
        lax.optimization_barrier(jnp.int32(1)),
        lambda i, carry: sum_over_head(partial_x, partial_y),
        (jnp.zeros((TOK, HD), BF16), jnp.zeros((TOK, HD), BF16)),
    )
    x1 = shift(x0, 1)
    x2 = shift(x0, 2)
    shard = lax.axis_index("seq").astype(jnp.int32)[None]
    tables = [jnp.asarray(t) for t in rope_tables(lax.axis_size("seq"))]
    query_grad, own, back1, back2, sketches = attention(
        shard, q_raw, d_out, k_raw, values, kv1, kv2, (x0, x1, x2, y0), q_gain, k_gain, tables
    )
    got2 = shift(back2, -2)
    got1 = shift(back1, -1)
    shards = lax.axis_size("seq")
    pieces = lax.all_to_all(sketches.reshape(shards, HD // shards, 12 * HD), "seq", 0, 0, tiled=True)
    total = jnp.sum(pieces.astype(F32), axis=0)
    kv_grad = (own + got1.astype(F32) + got2.astype(F32)).astype(BF16)

    q_cols, kv_cols = 4 * HD, 2 * HD
    return (
        query_grad,
        kv_grad[:, :kv_cols],
        kv_grad[:, kv_cols:],
        total[:, :q_cols],
        total[:, q_cols : q_cols + kv_cols],
        total[:, q_cols + kv_cols : q_cols + 2 * kv_cols],
        total[:, q_cols + 2 * kv_cols :],
    )


def solution(mesh):
    split = P("seq", "head")
    in_specs = (split, P("head", None), split, P("head", None), split, split, split, split, P(), P())
    return jax.shard_map(
        per_device, mesh=mesh, in_specs=in_specs, out_specs=(split,) * 7, check_vma=False
    )
```

```python
import jax
import jax.numpy as jnp
import numpy as np
from jax import lax
from jax.experimental import pallas as pl
from jax.experimental.pallas import tpu as pltpu
from jax.sharding import PartitionSpec as P

WINDOW = 1024
HD = 128
TOK = 512
QT = 256
KB = 256
ATTN_VMEM = 60 << 20
SPAN = 1536
NBLK = 5
score_scale = 168.0 ** (-0.5)
LOG2E = 1.4426950408889634
epsilon = 1e-06
rope_base = 10000.0
F32 = jnp.float32
BF16 = jnp.bfloat16


def rope_tables(shards):
    freq = rope_base ** (-(np.arange(64, dtype=np.float64) * 2.0 / HD))
    freq = np.concatenate([freq, freq])[None, :]
    base = ((np.arange(shards + 2) - 2) * TOK).astype(np.float64)[:, None] * freq
    local = np.arange(TOK, dtype=np.float64)[:, None] * freq
    pad = (-base.shape[0]) % 8
    base = np.pad(base, ((0, pad), (0, 0)))
    tables = [np.cos(base), np.sin(base), np.cos(local), np.sin(local)]
    return [t.astype(np.float32) for t in tables]


def norm_scale(raw):
    return lax.rsqrt(jnp.mean(raw * raw, axis=-1, keepdims=True) + epsilon)


def rope_forward(normed, cos, sin_signed):
    return normed * cos + pltpu.roll(normed, 64, 1) * sin_signed


def prep_back(raw, gain, cos, sin_signed, grad):
    r = norm_scale(raw)
    d_norm = (grad * cos - pltpu.roll(grad, 64, 1) * sin_signed) * gain
    return r * d_norm - raw * ((r * r * r) * jnp.mean(raw * d_norm, axis=-1, keepdims=True))


def mm(a, b):
    return lax.dot_general(a, b, (((1,), (0,)), ((), ())), preferred_element_type=F32)


def mm_t(a, b):
    return lax.dot_general(a, b, (((1,), (1,)), ((), ())), preferred_element_type=F32)


def attention_kernel(
    shard_ref, q_ref, do_ref, k0_ref, v0_ref, kv1_ref, kv2_ref,
    x0_ref, x1_ref, x2_ref, y_ref, qg_ref, kg_ref, cb_ref, sb_ref, cl_ref, sl_ref,
    qgrad_ref, own_ref, back1_ref, back2_ref, sk_ref,
    kp, vx, cos, sin, e_sc, dp_sc, dkt, dvt, xt, yt, skq, sko,
):
    tile = pl.program_id(1)
    shard = shard_ref[0]
    k_lanes = pl.ds(pl.multiple_of(pl.program_id(0) * HD, HD), HD)
    v_lanes = pl.ds(pl.multiple_of(pl.program_id(0) * HD + 2 * HD, HD), HD)
    k_parts = (kv2_ref.at[:, k_lanes], kv1_ref.at[:, k_lanes], k0_ref)
    v_parts = (kv2_ref.at[:, v_lanes], kv1_ref.at[:, v_lanes], v0_ref)

    @pl.when((pl.program_id(0) == 0) & (tile == 0))
    def _():
        lane = lax.broadcasted_iota(jnp.int32, (1, HD), 1)
        sign = jnp.where(lane < HD // 2, -1.0, 1.0)
        for part in range(3):
            cb = cb_ref[pl.ds(shard + part, 1), :]
            sb = sb_ref[pl.ds(shard + part, 1), :]
            rows = slice(part * TOK, (part + 1) * TOK)
            cos[rows, :] = cb * cl_ref[...] - sb * sl_ref[...]
            sin[rows, :] = (sb * cl_ref[...] + cb * sl_ref[...]) * sign

        for part, x_ref in enumerate((x2_ref, x1_ref, x0_ref)):
            xt[:, part * TOK : (part + 1) * TOK] = x_ref[...].astype(F32).T.astype(BF16)
        yt[...] = y_ref[...].astype(F32).T.astype(BF16)

    @pl.when(tile == 0)
    def _():
        skq[...] = jnp.zeros_like(skq)
        sko[...] = jnp.zeros_like(sko)
        for part, (k_ref, v_ref) in enumerate(zip(k_parts, v_parts)):
            rows = slice(part * TOK, (part + 1) * TOK)
            raw = k_ref[...].astype(F32)
            normed = raw * norm_scale(raw) * kg_ref[...]
            kp[rows, :] = rope_forward(normed, cos[rows, :], sin[rows, :]).astype(BF16)
            vx[rows, :] = v_ref[...]
        dkt[...] = jnp.zeros_like(dkt)
        dvt[...] = jnp.zeros_like(dvt)

    q_rows = pl.ds(pl.multiple_of(2 * TOK + tile * QT, QT), QT)
    cos_q = cos[q_rows, :]
    sin_q = sin[q_rows, :]
    q_parts = []
    for g in range(2):
        raw = q_ref[:, g * HD : (g + 1) * HD].astype(F32)
        normed = raw * norm_scale(raw) * qg_ref[...]
        q_parts.append(rope_forward(normed, cos_q, sin_q))
    q = jnp.concatenate(q_parts, axis=0)
    d_out = jnp.concatenate([do_ref[:, :HD], do_ref[:, HD:]], axis=0)
    q_low = q.astype(BF16)
    q_t = q.T.astype(BF16)
    do_t = d_out.astype(F32).T.astype(BF16)

    rows_i = lax.broadcasted_iota(jnp.int32, (QT, KB), 0)
    cols_i = lax.broadcasted_iota(jnp.int32, (QT, KB), 1)
    lower = (cols_i <= rows_i).astype(F32)
    upper = 1.0 - lower
    lower = jnp.concatenate([lower, lower], axis=0)
    upper = jnp.concatenate([upper, upper], axis=0)

    l_acc = jnp.zeros((2 * QT, HD), F32)
    u_acc = jnp.zeros((2 * QT, HD), F32)
    for b in range(NBLK):
        at = pl.ds(pl.multiple_of(tile * QT + b * KB, KB), KB)
        cols = slice(b * KB, (b + 1) * KB)
        s = mm_t(q_low, kp[at, :])
        e = jnp.exp2(s * (score_scale * LOG2E))
        key_shard = shard - 2 + (tile * QT + b * KB) // TOK
        if b == 0:
            e = e * (upper * jnp.where(key_shard >= 0, 1.0, 0.0))
        elif b == NBLK - 1:
            e = e * lower
        else:
            e = e * jnp.where(key_shard >= 0, 1.0, 0.0)
        dp = mm_t(d_out, vx[at, :])
        ed = e * dp
        l_acc = l_acc + e[:, :HD] + e[:, HD:]
        u_acc = u_acc + ed[:, :HD] + ed[:, HD:]
        e_sc[:, cols] = e
        dp_sc[:, cols] = dp
    inv = 1.0 / jnp.sum(l_acc, axis=-1, keepdims=True)
    delta = jnp.sum(u_acc, axis=-1, keepdims=True) * inv

    out = jnp.zeros((2 * QT, HD), F32)
    dq = jnp.zeros((2 * QT, HD), F32)
    for b in range(NBLK):
        at = pl.ds(pl.multiple_of(tile * QT + b * KB, KB), KB)
        cols = slice(b * KB, (b + 1) * KB)
        p = e_sc[:, cols] * inv
        ds = (p * (dp_sc[:, cols] - delta)).astype(BF16)
        p = p.astype(BF16)
        out = out + mm(p, vx[at, :])
        dq = dq + mm(ds, kp[at, :])
        dvt[:, at] += mm(do_t, p)
        dkt[:, at] += mm(q_t, ds)
    x_tile = xt[:, q_rows]
    y_tile = yt[:, pl.ds(pl.multiple_of(tile * QT, QT), QT)]
    for g in range(2):
        rows = slice(g * QT, (g + 1) * QT)
        lanes = slice(g * HD, (g + 1) * HD)
        raw = q_ref[:, lanes].astype(F32)
        q_grad = prep_back(raw, qg_ref[...], cos_q, sin_q, dq[rows] * score_scale).astype(BF16)
        qgrad_ref[:, lanes] = q_grad
        skq[:, lanes] += mm(x_tile, q_grad)
        sko[:, lanes] += mm(y_tile, out[rows].astype(BF16))

    @pl.when(tile == 1)
    def _():
        sk_k = jnp.zeros((HD, HD), F32)
        sk_v = jnp.zeros((HD, HD), F32)
        for part, k_ref in enumerate(k_parts):
            rows = slice(part * TOK, (part + 1) * TOK)
            raw = k_ref[...].astype(F32)
            dk = prep_back(
                raw, kg_ref[...], cos[rows, :], sin[rows, :], dkt[:, rows].T * score_scale
            )
            dv = dvt[:, rows].T
            sk_k = sk_k + mm(xt[:, rows], dk.astype(BF16))
            sk_v = sk_v + mm(xt[:, rows], dv.astype(BF16))
            target = (back2_ref, back1_ref, own_ref)[part]
            target[:, k_lanes] = dk.astype(target.dtype)
            target[:, v_lanes] = dv.astype(target.dtype)
        head = pl.program_id(0)
        sk_ref[:, pl.ds(pl.multiple_of(head * 2 * HD, 2 * HD), 2 * HD)] = skq[...].astype(BF16)
        sk_ref[:, pl.ds(pl.multiple_of(head * HD + 4 * HD, HD), HD)] = sk_k.astype(BF16)
        sk_ref[:, pl.ds(pl.multiple_of(head * HD + 6 * HD, HD), HD)] = sk_v.astype(BF16)
        sk_ref[:, pl.ds(pl.multiple_of(head * 2 * HD + 8 * HD, 2 * HD), 2 * HD)] = sko[...].astype(BF16)


def attention(shard, q_raw, d_out, k_raw, values, kv1, kv2, sketches, q_gain, k_gain, tables):
    whole = lambda a: pl.BlockSpec(a.shape, lambda h, t: (0,) * a.ndim)
    tile_spec = pl.BlockSpec((QT, 2 * HD), lambda h, t: (t, h))
    k_spec = pl.BlockSpec((TOK, HD), lambda h, t: (0, h))
    consts = [kv1, kv2, *sketches, q_gain[None, :], k_gain[None, :]] + tables
    q_shape = jax.ShapeDtypeStruct((TOK, 4 * HD), BF16)
    kv_shape = jax.ShapeDtypeStruct((TOK, 4 * HD), BF16)
    own_shape = jax.ShapeDtypeStruct((TOK, 4 * HD), F32)
    sk_shape = jax.ShapeDtypeStruct((HD, 12 * HD), BF16)
    return pl.pallas_call(
        attention_kernel,
        grid=(2, 2),
        in_specs=[pl.BlockSpec(memory_space=pltpu.SMEM), tile_spec, tile_spec, k_spec, k_spec]
        + [whole(a) for a in consts],
        out_specs=[tile_spec, whole(own_shape), whole(kv_shape), whole(kv_shape), whole(sk_shape)],
        out_shape=[q_shape, own_shape, kv_shape, kv_shape, sk_shape],
        scratch_shapes=[
            pltpu.VMEM((SPAN, HD), BF16),
            pltpu.VMEM((SPAN, HD), BF16),
            pltpu.VMEM((SPAN, HD), F32),
            pltpu.VMEM((SPAN, HD), F32),
            pltpu.VMEM((2 * QT, NBLK * KB), F32),
            pltpu.VMEM((2 * QT, NBLK * KB), F32),
            pltpu.VMEM((HD, SPAN), F32),
            pltpu.VMEM((HD, SPAN), F32),
            pltpu.VMEM((HD, SPAN), BF16),
            pltpu.VMEM((HD, TOK), BF16),
            pltpu.VMEM((HD, 2 * HD), F32),
            pltpu.VMEM((HD, 2 * HD), F32),
        ],
        compiler_params=pltpu.CompilerParams(vmem_limit_bytes=ATTN_VMEM),
        cost_estimate=pl.CostEstimate(
            flops=6 * 4 * 2 * TOK * SPAN * HD, bytes_accessed=6 << 20, transcendentals=4 * TOK * SPAN
        ),
    )(shard, q_raw, d_out, k_raw, values, *consts)


def shift(x, by):
    count = lax.axis_size("seq")
    pairs = [(i, i + by) for i in range(count) if 0 <= i + by < count]
    return lax.ppermute(x, "seq", pairs)


def swap(x, bit):
    count = lax.axis_size("head")
    return lax.ppermute(x, "head", [(i, i ^ bit) for i in range(count)])


def pair_swap(x):
    count = lax.axis_size("seq")
    return lax.ppermute(x, "seq", [(i, i ^ 1) for i in range(count)])


def one_turn(step, example):
    turns = lax.optimization_barrier(jnp.int32(1))
    zeros = jax.tree.map(lambda a: jnp.zeros(a.shape, a.dtype), example)
    return lax.fori_loop(0, turns, lambda i, carry: step(), zeros)


def per_device(
    layer_input, omega_in, upstream, omega_out, q_raw, k_raw, values, d_out, q_gain, k_gain
):
    kv = jnp.concatenate([k_raw, values], axis=1)
    kv, layer_input, upstream = lax.optimization_barrier((kv, layer_input, upstream))
    odd = lax.axis_index("seq") % 2 == 1
    first = lax.axis_index("head") % 2 == 0
    kv2 = shift(kv, 2)
    partial_x = jnp.dot(layer_input, omega_in, preferred_element_type=F32)
    partial_y = jnp.dot(upstream, omega_out, preferred_element_type=F32)
    wide = jax.ShapeDtypeStruct((TOK, HD), F32)
    low = jax.ShapeDtypeStruct((TOK, HD), BF16)

    def sum_near():
        got = swap(jnp.where(first, partial_y, partial_x).astype(BF16), 1)
        total = jnp.where(first, partial_x, partial_y) + got.astype(F32)
        return total + swap(total.astype(BF16), 2).astype(F32)

    half = one_turn(sum_near, wide)
    kv1 = pair_swap(jnp.where(odd, kv2, kv))

    def sum_far():
        mine = (half + swap(half.astype(BF16), 4).astype(F32)).astype(BF16)
        other = swap(mine, 1)
        return jnp.where(first, mine, other), jnp.where(first, other, mine)

    x0, y0 = one_turn(sum_far, (low, low))
    x1 = shift(x0, 1)
    x2 = shift(x0, 2)
    shard = lax.axis_index("seq").astype(jnp.int32)[None]
    tables = [jnp.asarray(t) for t in rope_tables(lax.axis_size("seq"))]
    query_grad, own, back1, back2, sketches = attention(
        shard, q_raw, d_out, k_raw, values, kv1, kv2, (x0, x1, x2, y0), q_gain, k_gain, tables
    )
    near = pair_swap(back1).astype(F32)
    back2 = back2.astype(F32)
    far = shift(jnp.where(odd, back2 + near, back2).astype(BF16), -2)
    shards = lax.axis_size("seq")
    pieces = lax.all_to_all(sketches.reshape(shards, HD // shards, 12 * HD), "seq", 0, 0, tiled=True)
    total = jnp.sum(pieces.astype(F32), axis=0)
    kv_grad = (own + jnp.where(odd, 0.0, near) + far.astype(F32)).astype(BF16)

    q_cols, kv_cols = 4 * HD, 2 * HD
    return (
        query_grad,
        kv_grad[:, :kv_cols],
        kv_grad[:, kv_cols:],
        total[:, :q_cols],
        total[:, q_cols : q_cols + kv_cols],
        total[:, q_cols + kv_cols : q_cols + 2 * kv_cols],
        total[:, q_cols + 2 * kv_cols :],
    )


def solution(mesh):
    split = P("seq", "head")
    in_specs = (split, P("head", None), split, P("head", None), split, split, split, split, P(), P())
    return jax.shard_map(
        per_device, mesh=mesh, in_specs=in_specs, out_specs=(split,) * 7, check_vma=False
    )
```

```python
import jax
import jax.numpy as jnp
import numpy as np
from jax import lax
from jax.experimental import pallas as pl
from jax.experimental.pallas import tpu as pltpu
from jax.sharding import PartitionSpec as P

WINDOW = 1024
HD = 128
TOK = 512
QT = 256
KB = 256
ATTN_VMEM = 60 << 20
SPAN = 1536
NBLK = 5
score_scale = 168.0 ** (-0.5)
LOG2E = 1.4426950408889634
epsilon = 1e-06
rope_base = 10000.0
F32 = jnp.float32
BF16 = jnp.bfloat16


def rope_tables(shards):
    freq = rope_base ** (-(np.arange(64, dtype=np.float64) * 2.0 / HD))
    freq = np.concatenate([freq, freq])[None, :]
    base = ((np.arange(shards + 2) - 2) * TOK).astype(np.float64)[:, None] * freq
    local = np.arange(TOK, dtype=np.float64)[:, None] * freq
    pad = (-base.shape[0]) % 8
    base = np.pad(base, ((0, pad), (0, 0)))
    tables = [np.cos(base), np.sin(base), np.cos(local), np.sin(local)]
    return [t.astype(np.float32) for t in tables]


def lane_mean(x):
    high = x.astype(BF16)
    low = (x - high.astype(F32)).astype(BF16)
    ones = jnp.full((HD, HD), 1.0 / HD, BF16)
    return mm(high, ones) + mm(low, ones)


def norm_scale(raw):
    return lax.rsqrt(lane_mean(raw * raw) + epsilon)


def rope_forward(normed, cos, sin_signed):
    return normed * cos + pltpu.roll(normed, 64, 1) * sin_signed


def prep_back(raw, r, gain, cos, sin_signed, grad):
    d_norm = (grad * cos - pltpu.roll(grad, 64, 1) * sin_signed) * gain
    return r * d_norm - raw * ((r * r * r) * lane_mean(raw * d_norm))


def mm(a, b):
    return lax.dot_general(a, b, (((1,), (0,)), ((), ())), preferred_element_type=F32)


def mm_t(a, b):
    return lax.dot_general(a, b, (((1,), (1,)), ((), ())), preferred_element_type=F32)


N_IN = 10


def attention_kernel(
    shard_ref, q_hbm, do_hbm, k0_hbm, v0_hbm, kv1_hbm, kv2_hbm, x0_hbm, x1_hbm, x2_hbm, y_hbm,
    qg_ref, kg_ref, cb_ref, sb_ref, cl_ref, sl_ref,
    qgrad_hbm, own_hbm, back1_hbm, back2_hbm, sk_ref,
    q_ref, do_ref, k0_ref, v0_ref, kv1_ref, kv2_ref, x0_ref, x1_ref, x2_ref, y_ref,
    qgrad_ref, own_ref, back1_ref, back2_ref,
    kp, vx, r_k, cos, sin, e_sc, dp_sc, dkt, dvt, xt, yt, skq, sko, in_sems, out_sems,
):
    sources = (k0_hbm, kv2_hbm, kv1_hbm, v0_hbm, x0_hbm, x1_hbm, x2_hbm, y_hbm, q_hbm, do_hbm)
    targets = (k0_ref, kv2_ref, kv1_ref, v0_ref, x0_ref, x1_ref, x2_ref, y_ref, q_ref, do_ref)
    loads = [pltpu.make_async_copy(a, b, in_sems.at[n]) for n, (a, b) in enumerate(zip(sources, targets))]
    for load in loads:
        load.start()
    shard = shard_ref[0]
    lane = lax.broadcasted_iota(jnp.int32, (1, HD), 1)
    sign = jnp.where(lane < HD // 2, -1.0, 1.0)
    for part in range(3):
        cb = cb_ref[pl.ds(shard + part, 1), :]
        sb = sb_ref[pl.ds(shard + part, 1), :]
        rows = slice(part * TOK, (part + 1) * TOK)
        cos[rows, :] = cb * cl_ref[...] - sb * sl_ref[...]
        sin[rows, :] = (sb * cl_ref[...] + cb * sl_ref[...]) * sign
    for load in loads:
        load.wait()
    for part, x_ref in enumerate((x2_ref, x1_ref, x0_ref)):
        xt[:, part * TOK : (part + 1) * TOK] = x_ref[...].astype(F32).T.astype(BF16)
    yt[...] = y_ref[...].astype(F32).T.astype(BF16)
    refs = (
        shard, q_ref, do_ref, k0_ref, v0_ref, kv1_ref, kv2_ref, qg_ref, kg_ref,
        qgrad_ref, own_ref, back1_ref, back2_ref, sk_ref,
        kp, vx, r_k, cos, sin, e_sc, dp_sc, dkt, dvt, xt, yt, skq, sko,
    )

    def stores(head):
        lanes = pl.ds(pl.multiple_of(head * 2 * HD, 2 * HD), 2 * HD)
        out = [(qgrad_ref.at[:, lanes], qgrad_hbm.at[:, lanes])]
        for kind in range(2):
            lanes = pl.ds(pl.multiple_of(head * HD + kind * 2 * HD, HD), HD)
            for a, b in ((own_ref, own_hbm), (back1_ref, back1_hbm), (back2_ref, back2_hbm)):
                out.append((a.at[:, lanes], b.at[:, lanes]))
        return [pltpu.make_async_copy(a, b, out_sems.at[head, n]) for n, (a, b) in enumerate(out)]

    @pl.loop(0, 4)
    def _(step):
        head = step // 2
        attention_step(head, step % 2, *refs)

        @pl.when(step % 2 == 1)
        def _():
            for store in stores(head):
                store.start()

    for head in range(2):
        for store in stores(head):
            store.wait()


def attention_step(
    head, tile, shard, q_ref, do_ref, k0_ref, v0_ref, kv1_ref, kv2_ref, qg_ref, kg_ref,
    qgrad_ref, own_ref, back1_ref, back2_ref, sk_ref,
    kp, vx, r_k, cos, sin, e_sc, dp_sc, dkt, dvt, xt, yt, skq, sko,
):
    k_lanes = pl.ds(pl.multiple_of(head * HD, HD), HD)
    v_lanes = pl.ds(pl.multiple_of(head * HD + 2 * HD, HD), HD)
    k_parts = (kv2_ref.at[:, k_lanes], kv1_ref.at[:, k_lanes], k0_ref.at[:, k_lanes])
    v_parts = (kv2_ref.at[:, v_lanes], kv1_ref.at[:, v_lanes], v0_ref.at[:, k_lanes])

    @pl.when(tile == 0)
    def _():
        skq[...] = jnp.zeros_like(skq)
        sko[...] = jnp.zeros_like(sko)
        for part, (k_ref, v_ref) in enumerate(zip(k_parts, v_parts)):
            rows = slice(part * TOK, (part + 1) * TOK)
            raw = k_ref[...].astype(F32)
            r = norm_scale(raw)
            r_k[rows, :] = r
            normed = raw * r * kg_ref[...]
            kp[rows, :] = rope_forward(normed, cos[rows, :], sin[rows, :]).astype(BF16)
            vx[rows, :] = v_ref[...]
        dkt[...] = jnp.zeros_like(dkt)
        dvt[...] = jnp.zeros_like(dvt)

    tile_rows = pl.ds(pl.multiple_of(tile * QT, QT), QT)
    q_rows = pl.ds(pl.multiple_of(2 * TOK + tile * QT, QT), QT)
    q_lanes = [pl.ds(pl.multiple_of(head * 2 * HD + g * HD, HD), HD) for g in range(2)]
    cos_q = cos[q_rows, :]
    sin_q = sin[q_rows, :]
    q_parts = []
    r_parts = []
    for lanes in q_lanes:
        raw = q_ref[tile_rows, lanes].astype(F32)
        r_parts.append(norm_scale(raw))
        q_parts.append(rope_forward(raw * r_parts[-1] * qg_ref[...], cos_q, sin_q))
    q = jnp.concatenate(q_parts, axis=0)
    d_out = jnp.concatenate([do_ref[tile_rows, lanes] for lanes in q_lanes], axis=0)
    q_low = q.astype(BF16)
    q_t = q.T.astype(BF16)
    do_t = d_out.astype(F32).T.astype(BF16)

    rows_i = lax.broadcasted_iota(jnp.int32, (2 * QT, KB), 0) % QT
    cols_i = lax.broadcasted_iota(jnp.int32, (2 * QT, KB), 1)

    l_acc = jnp.zeros((2 * QT, HD), F32)
    u_acc = jnp.zeros((2 * QT, HD), F32)
    for b in range(NBLK):
        at = pl.ds(pl.multiple_of(tile * QT + b * KB, KB), KB)
        cols = slice(b * KB, (b + 1) * KB)
        s = mm_t(q_low, kp[at, :])
        e = jnp.exp2(s * (score_scale * LOG2E))
        key_shard = shard - 2 + (tile * QT + b * KB) // TOK
        if b == 0:
            e = jnp.where((cols_i > rows_i) & (key_shard >= 0), e, 0.0)
        elif b == NBLK - 1:
            e = jnp.where(cols_i <= rows_i, e, 0.0)
        else:
            e = e * jnp.where(key_shard >= 0, 1.0, 0.0)
        dp = mm_t(d_out, vx[at, :])
        ed = e * dp
        l_acc = l_acc + e[:, :HD] + e[:, HD:]
        u_acc = u_acc + ed[:, :HD] + ed[:, HD:]
        e_sc[:, cols] = e
        dp_sc[:, cols] = dp
    inv = 1.0 / jnp.sum(l_acc, axis=-1, keepdims=True)
    delta = jnp.sum(u_acc, axis=-1, keepdims=True) * inv

    out = jnp.zeros((2 * QT, HD), F32)
    dq = jnp.zeros((2 * QT, HD), F32)
    for b in range(NBLK):
        at = pl.ds(pl.multiple_of(tile * QT + b * KB, KB), KB)
        cols = slice(b * KB, (b + 1) * KB)
        p = e_sc[:, cols] * inv
        ds = (p * (dp_sc[:, cols] - delta)).astype(BF16)
        p = p.astype(BF16)
        out = out + mm(p, vx[at, :])
        dq = dq + mm(ds, kp[at, :])
        dvt[:, at] += mm(do_t, p)
        dkt[:, at] += mm(q_t, ds)
    x_tile = xt[:, q_rows]
    y_tile = yt[:, tile_rows]
    for g in range(2):
        rows = slice(g * QT, (g + 1) * QT)
        lanes = slice(g * HD, (g + 1) * HD)
        raw = q_ref[tile_rows, q_lanes[g]].astype(F32)
        q_grad = prep_back(raw, r_parts[g], qg_ref[...], cos_q, sin_q, dq[rows] * score_scale).astype(BF16)
        qgrad_ref[tile_rows, q_lanes[g]] = q_grad
        skq[:, lanes] += mm(x_tile, q_grad)
        sko[:, lanes] += mm(y_tile, out[rows].astype(BF16))

    @pl.when(tile == 1)
    def _():
        sk_k = jnp.zeros((HD, HD), F32)
        sk_v = jnp.zeros((HD, HD), F32)
        for part, k_ref in enumerate(k_parts):
            rows = slice(part * TOK, (part + 1) * TOK)
            raw = k_ref[...].astype(F32)
            dk = prep_back(
                raw, r_k[rows, :], kg_ref[...], cos[rows, :], sin[rows, :], dkt[:, rows].T * score_scale
            )
            dv = dvt[:, rows].T
            sk_k = sk_k + mm(xt[:, rows], dk.astype(BF16))
            sk_v = sk_v + mm(xt[:, rows], dv.astype(BF16))
            target = (back2_ref, back1_ref, own_ref)[part]
            target[:, k_lanes] = dk.astype(target.dtype)
            target[:, v_lanes] = dv.astype(target.dtype)
        sk_ref[:, pl.ds(pl.multiple_of(head * 2 * HD, 2 * HD), 2 * HD)] = skq[...].astype(BF16)
        sk_ref[:, pl.ds(pl.multiple_of(head * HD + 4 * HD, HD), HD)] = sk_k.astype(BF16)
        sk_ref[:, pl.ds(pl.multiple_of(head * HD + 6 * HD, HD), HD)] = sk_v.astype(BF16)
        sk_ref[:, pl.ds(pl.multiple_of(head * 2 * HD + 8 * HD, 2 * HD), 2 * HD)] = sko[...].astype(BF16)


def attention(shard, q_raw, d_out, k_raw, values, kv1, kv2, sketches, q_gain, k_gain, tables):
    vmem = pl.BlockSpec(memory_space=pltpu.VMEM)
    arrays = [q_raw, d_out, k_raw, values, kv1, kv2, *sketches, q_gain[None, :], k_gain[None, :]] + tables
    return pl.pallas_call(
        attention_kernel,
        in_specs=[pl.BlockSpec(memory_space=pltpu.SMEM)] + [pl.BlockSpec(memory_space=pl.ANY)] * N_IN + [vmem] * 6,
        out_specs=[pl.BlockSpec(memory_space=pl.ANY)] * 4 + [vmem],
        out_shape=[
            jax.ShapeDtypeStruct((TOK, 4 * HD), BF16),
            jax.ShapeDtypeStruct((TOK, 4 * HD), F32),
            jax.ShapeDtypeStruct((TOK, 4 * HD), BF16),
            jax.ShapeDtypeStruct((TOK, 4 * HD), BF16),
            jax.ShapeDtypeStruct((HD, 12 * HD), BF16),
        ],
        scratch_shapes=[pltpu.VMEM(a.shape, a.dtype) for a in arrays[:N_IN]] + [
            pltpu.VMEM((TOK, 4 * HD), BF16),
            pltpu.VMEM((TOK, 4 * HD), F32),
            pltpu.VMEM((TOK, 4 * HD), BF16),
            pltpu.VMEM((TOK, 4 * HD), BF16),
            pltpu.VMEM((SPAN, HD), BF16),
            pltpu.VMEM((SPAN, HD), BF16),
            pltpu.VMEM((SPAN, HD), F32),
            pltpu.VMEM((SPAN, HD), F32),
            pltpu.VMEM((SPAN, HD), F32),
            pltpu.VMEM((2 * QT, NBLK * KB), F32),
            pltpu.VMEM((2 * QT, NBLK * KB), F32),
            pltpu.VMEM((HD, SPAN), F32),
            pltpu.VMEM((HD, SPAN), F32),
            pltpu.VMEM((HD, SPAN), BF16),
            pltpu.VMEM((HD, TOK), BF16),
            pltpu.VMEM((HD, 2 * HD), F32),
            pltpu.VMEM((HD, 2 * HD), F32),
            pltpu.SemaphoreType.DMA((N_IN,)),
            pltpu.SemaphoreType.DMA((2, 7)),
        ],
        compiler_params=pltpu.CompilerParams(vmem_limit_bytes=ATTN_VMEM),
        cost_estimate=pl.CostEstimate(
            flops=6 * 4 * 2 * TOK * SPAN * HD, bytes_accessed=6 << 20, transcendentals=4 * TOK * SPAN
        ),
    )(shard, *arrays)


def shift(x, by):
    count = lax.axis_size("seq")
    pairs = [(i, i + by) for i in range(count) if 0 <= i + by < count]
    return lax.ppermute(x, "seq", pairs)


def swap(x, bit):
    count = lax.axis_size("head")
    return lax.ppermute(x, "head", [(i, i ^ bit) for i in range(count)])


def pair_swap(x):
    count = lax.axis_size("seq")
    return lax.ppermute(x, "seq", [(i, i ^ 1) for i in range(count)])


def one_turn(step, start):
    return lax.fori_loop(0, lax.optimization_barrier(jnp.int32(1)), lambda i, carry: step(), start)


def per_device(
    layer_input, omega_in, upstream, omega_out, q_raw, k_raw, values, d_out, q_gain, k_gain
):
    kv = jnp.concatenate([k_raw, values], axis=1)
    kv, layer_input, upstream = lax.optimization_barrier((kv, layer_input, upstream))
    odd = lax.axis_index("seq") % 2 == 1
    first = lax.axis_index("head") % 2 == 0
    kv2 = shift(kv, 2)
    partial_x = jnp.dot(layer_input, omega_in, preferred_element_type=F32)
    partial_y = jnp.dot(upstream, omega_out, preferred_element_type=F32)

    def sum_near():
        got = swap(jnp.where(first, partial_y, partial_x).astype(BF16), 1)
        total = jnp.where(first, partial_x, partial_y) + got.astype(F32)
        return total + swap(total.astype(BF16), 2).astype(F32)

    half = one_turn(sum_near, partial_x)
    kv1 = pair_swap(jnp.where(odd, kv2, kv))

    def sum_far():
        mine = (half + swap(half.astype(BF16), 6).astype(F32)).astype(BF16)
        other = swap(mine, 1)
        return jnp.where(first, mine, other), jnp.where(first, other, mine)

    x0, y0 = sum_far()
    x1 = shift(x0, 1)
    x2 = shift(x0, 2)
    shard = lax.axis_index("seq").astype(jnp.int32)[None]
    tables = [jnp.asarray(t) for t in rope_tables(lax.axis_size("seq"))]
    query_grad, own, back1, back2, sketches = attention(
        shard, q_raw, d_out, k_raw, values, kv1, kv2, (x0, x1, x2, y0), q_gain, k_gain, tables
    )
    near = pair_swap(back1).astype(F32)
    back2 = back2.astype(F32)
    far = shift(jnp.where(odd, back2 + near, back2).astype(BF16), -2)
    shards = lax.axis_size("seq")
    pieces = lax.all_to_all(sketches.reshape(shards, HD // shards, 12 * HD), "seq", 0, 0, tiled=True)
    total = jnp.sum(pieces.astype(F32), axis=0)
    kv_grad = (own + jnp.where(odd, 0.0, near) + far.astype(F32)).astype(BF16)

    q_cols, kv_cols = 4 * HD, 2 * HD
    return (
        query_grad,
        kv_grad[:, :kv_cols],
        kv_grad[:, kv_cols:],
        total[:, :q_cols],
        total[:, q_cols : q_cols + kv_cols],
        total[:, q_cols + kv_cols : q_cols + 2 * kv_cols],
        total[:, q_cols + 2 * kv_cols :],
    )


def solution(mesh):
    split = P("seq", "head")
    in_specs = (split, P("head", None), split, P("head", None), split, split, split, split, P(), P())
    return jax.shard_map(
        per_device, mesh=mesh, in_specs=in_specs, out_specs=(split,) * 7, check_vma=False
    )
```

```python
import jax
import jax.numpy as jnp
import numpy as np
from jax import lax
from jax.experimental import pallas as pl
from jax.experimental.pallas import tpu as pltpu
from jax.sharding import PartitionSpec as P

WINDOW = 1024
HD = 128
TOK = 512
QT = 256
KB = 256
ATTN_VMEM = 60 << 20
SPAN = 1536
NBLK = 5
score_scale = 168.0 ** (-0.5)
LOG2E = 1.4426950408889634
epsilon = 1e-06
rope_base = 10000.0
F32 = jnp.float32
BF16 = jnp.bfloat16


def rope_tables(shards):
    freq = rope_base ** (-(np.arange(64, dtype=np.float64) * 2.0 / HD))
    freq = np.concatenate([freq, freq])[None, :]
    base = ((np.arange(shards + 2) - 2) * TOK).astype(np.float64)[:, None] * freq
    local = np.arange(TOK, dtype=np.float64)[:, None] * freq
    pad = (-base.shape[0]) % 8
    base = np.pad(base, ((0, pad), (0, 0)))
    tables = [np.cos(base), np.sin(base), np.cos(local), np.sin(local)]
    return [t.astype(np.float32) for t in tables]


def lane_mean(x):
    high = x.astype(BF16)
    low = (x - high.astype(F32)).astype(BF16)
    ones = jnp.full((HD, HD), 1.0 / HD, BF16)
    return mm(high, ones) + mm(low, ones)


def norm_scale(raw):
    return lax.rsqrt(lane_mean(raw * raw) + epsilon)


def rope_forward(normed, cos, sin_signed):
    return normed * cos + pltpu.roll(normed, 64, 1) * sin_signed


def prep_back(raw, r, gain, cos, sin_signed, grad):
    d_norm = (grad * cos - pltpu.roll(grad, 64, 1) * sin_signed) * gain
    return r * d_norm - raw * ((r * r * r) * lane_mean(raw * d_norm))


def mm(a, b):
    return lax.dot_general(a, b, (((1,), (0,)), ((), ())), preferred_element_type=F32)


def mm_t(a, b):
    return lax.dot_general(a, b, (((1,), (1,)), ((), ())), preferred_element_type=F32)


N_IN = 16


def attention_kernel(
    shard_ref, q_hbm, do_hbm, k0_hbm, v0_hbm, kv1_hbm, kv2_hbm, x0_hbm, x1_hbm, x2_hbm, y_hbm,
    qg_hbm, kg_hbm, cb_hbm, sb_hbm, cl_hbm, sl_hbm,
    qgrad_hbm, own_hbm, back1_hbm, back2_hbm, sk_hbm,
    q_ref, do_ref, k0_ref, v0_ref, kv1_ref, kv2_ref, x0_ref, x1_ref, x2_ref, y_ref,
    qg_ref, kg_ref, cb_ref, sb_ref, cl_ref, sl_ref,
    qgrad_ref, own_ref, back1_ref, back2_ref, sk_ref,
    kp, vx, r_k, cos, sin, e_sc, dp_sc, dkt, dvt, xt, yt, skq, sko, in_sems, out_sems,
):
    sources = (cb_hbm, sb_hbm, cl_hbm, sl_hbm, qg_hbm, kg_hbm) + (k0_hbm, kv2_hbm, kv1_hbm, v0_hbm, q_hbm, do_hbm, x0_hbm, x1_hbm, x2_hbm, y_hbm)
    targets = (cb_ref, sb_ref, cl_ref, sl_ref, qg_ref, kg_ref) + (k0_ref, kv2_ref, kv1_ref, v0_ref, q_ref, do_ref, x0_ref, x1_ref, x2_ref, y_ref)
    loads = [pltpu.make_async_copy(a, b, in_sems.at[n]) for n, (a, b) in enumerate(zip(sources, targets))]
    for load in loads:
        load.start()
    shard = shard_ref[0]
    for load in loads[:6]:
        load.wait()
    lane = lax.broadcasted_iota(jnp.int32, (1, HD), 1)
    sign = jnp.where(lane < HD // 2, -1.0, 1.0)
    for part in range(3):
        cb = cb_ref[pl.ds(shard + part, 1), :]
        sb = sb_ref[pl.ds(shard + part, 1), :]
        rows = slice(part * TOK, (part + 1) * TOK)
        cos[rows, :] = cb * cl_ref[...] - sb * sl_ref[...]
        sin[rows, :] = (sb * cl_ref[...] + cb * sl_ref[...]) * sign
    for load in loads[6:10]:
        load.wait()

    def wait_queries():
        for load in loads[10:12]:
            load.wait()

    def wait_sketches():
        for load in loads[12:]:
            load.wait()
        for part, x_ref in enumerate((x2_ref, x1_ref, x0_ref)):
            xt[:, part * TOK : (part + 1) * TOK] = x_ref[...].T
        yt[...] = y_ref[...].T

    refs = (
        shard, q_ref, do_ref, k0_ref, v0_ref, kv1_ref, kv2_ref, qg_ref, kg_ref,
        qgrad_ref, own_ref, back1_ref, back2_ref, sk_ref,
        kp, vx, r_k, cos, sin, e_sc, dp_sc, dkt, dvt, xt, yt, skq, sko,
    )

    def stores(head):
        lanes = pl.ds(pl.multiple_of(head * 2 * HD, 2 * HD), 2 * HD)
        out = [(qgrad_ref.at[:, lanes], qgrad_hbm.at[:, lanes])]
        for kind in range(2):
            lanes = pl.ds(pl.multiple_of(head * HD + kind * 2 * HD, HD), HD)
            for a, b in ((own_ref, own_hbm), (back1_ref, back1_hbm), (back2_ref, back2_hbm)):
                out.append((a.at[:, lanes], b.at[:, lanes]))
        return [pltpu.make_async_copy(a, b, out_sems.at[head, n]) for n, (a, b) in enumerate(out)]

    @pl.loop(0, 4)
    def _(step):
        head = step // 2
        attention_step(head, step % 2, wait_queries, wait_sketches, *refs)

        @pl.when(step % 2 == 1)
        def _():
            for store in stores(head):
                store.start()

    sketch_store = pltpu.make_async_copy(sk_ref, sk_hbm, out_sems.at[0, 7])
    sketch_store.start()
    for head in range(2):
        for store in stores(head):
            store.wait()
    sketch_store.wait()


def attention_step(
    head, tile, wait_queries, wait_sketches, shard, q_ref, do_ref, k0_ref, v0_ref, kv1_ref, kv2_ref, qg_ref, kg_ref,
    qgrad_ref, own_ref, back1_ref, back2_ref, sk_ref,
    kp, vx, r_k, cos, sin, e_sc, dp_sc, dkt, dvt, xt, yt, skq, sko,
):
    k_lanes = pl.ds(pl.multiple_of(head * HD, HD), HD)
    v_lanes = pl.ds(pl.multiple_of(head * HD + 2 * HD, HD), HD)
    k_parts = (kv2_ref.at[:, k_lanes], kv1_ref.at[:, k_lanes], k0_ref.at[:, k_lanes])
    v_parts = (kv2_ref.at[:, v_lanes], kv1_ref.at[:, v_lanes], v0_ref.at[:, k_lanes])

    @pl.when(tile == 0)
    def _():
        skq[...] = jnp.zeros_like(skq)
        sko[...] = jnp.zeros_like(sko)
        for part, (k_ref, v_ref) in enumerate(zip(k_parts, v_parts)):
            rows = slice(part * TOK, (part + 1) * TOK)
            raw = k_ref[...].astype(F32)
            r = norm_scale(raw)
            r_k[rows, :] = r
            normed = raw * r * kg_ref[...]
            kp[rows, :] = rope_forward(normed, cos[rows, :], sin[rows, :]).astype(BF16)
            vx[rows, :] = v_ref[...]
        dkt[...] = jnp.zeros_like(dkt)
        dvt[...] = jnp.zeros_like(dvt)

    pl.when((head == 0) & (tile == 0))(wait_queries)
    tile_rows = pl.ds(pl.multiple_of(tile * QT, QT), QT)
    q_rows = pl.ds(pl.multiple_of(2 * TOK + tile * QT, QT), QT)
    q_lanes = [pl.ds(pl.multiple_of(head * 2 * HD + g * HD, HD), HD) for g in range(2)]
    cos_q = cos[q_rows, :]
    sin_q = sin[q_rows, :]
    q_parts = []
    r_parts = []
    for lanes in q_lanes:
        raw = q_ref[tile_rows, lanes].astype(F32)
        r_parts.append(norm_scale(raw))
        q_parts.append(rope_forward(raw * r_parts[-1] * qg_ref[...], cos_q, sin_q))
    q = jnp.concatenate(q_parts, axis=0)
    d_out = jnp.concatenate([do_ref[tile_rows, lanes] for lanes in q_lanes], axis=0)
    q_low = q.astype(BF16)
    q_t = q_low.T
    do_t = d_out.T

    rows_i = lax.broadcasted_iota(jnp.int32, (2 * QT, KB), 0) & (QT - 1)
    cols_i = lax.broadcasted_iota(jnp.int32, (2 * QT, KB), 1)

    l_acc = jnp.zeros((2 * QT, HD), F32)
    u_acc = jnp.zeros((2 * QT, HD), F32)
    for b in range(NBLK):
        at = pl.ds(pl.multiple_of(tile * QT + b * KB, KB), KB)
        cols = slice(b * KB, (b + 1) * KB)
        s = mm_t(q_low, kp[at, :])
        e = jnp.exp2(s * (score_scale * LOG2E))
        key_shard = shard - 2 + (tile * QT + b * KB) // TOK
        if b == 0:
            e = jnp.where((cols_i > rows_i) & (key_shard >= 0), e, 0.0)
        elif b == NBLK - 1:
            e = jnp.where(cols_i <= rows_i, e, 0.0)
        else:
            e = e * jnp.where(key_shard >= 0, 1.0, 0.0)
        dp = mm_t(d_out, vx[at, :])
        ed = e * dp
        l_acc = l_acc + e[:, :HD] + e[:, HD:]
        u_acc = u_acc + ed[:, :HD] + ed[:, HD:]
        e_sc[:, cols] = e
        dp_sc[:, cols] = dp
    inv = 1.0 / jnp.sum(l_acc, axis=-1, keepdims=True)
    delta = jnp.sum(u_acc, axis=-1, keepdims=True) * inv

    out = jnp.zeros((2 * QT, HD), F32)
    dq = jnp.zeros((2 * QT, HD), F32)
    for b in range(NBLK):
        at = pl.ds(pl.multiple_of(tile * QT + b * KB, KB), KB)
        cols = slice(b * KB, (b + 1) * KB)
        p = e_sc[:, cols] * inv
        ds = (p * (dp_sc[:, cols] - delta)).astype(BF16)
        p = p.astype(BF16)
        out = out + mm(p, vx[at, :])
        dq = dq + mm(ds, kp[at, :])
        dvt[:, at] += mm(do_t, p)
        dkt[:, at] += mm(q_t, ds)
    pl.when((head == 0) & (tile == 0))(wait_sketches)
    x_tile = xt[:, q_rows]
    y_tile = yt[:, tile_rows]
    for g in range(2):
        rows = slice(g * QT, (g + 1) * QT)
        lanes = slice(g * HD, (g + 1) * HD)
        raw = q_ref[tile_rows, q_lanes[g]].astype(F32)
        q_grad = prep_back(raw, r_parts[g], qg_ref[...], cos_q, sin_q, dq[rows] * score_scale).astype(BF16)
        qgrad_ref[tile_rows, q_lanes[g]] = q_grad
        skq[:, lanes] += mm(x_tile, q_grad)
        sko[:, lanes] += mm(y_tile, out[rows].astype(BF16))

    @pl.when(tile == 1)
    def _():
        sk_k = jnp.zeros((HD, HD), F32)
        sk_v = jnp.zeros((HD, HD), F32)
        for part, k_ref in enumerate(k_parts):
            rows = slice(part * TOK, (part + 1) * TOK)
            raw = k_ref[...].astype(F32)
            dk = prep_back(
                raw, r_k[rows, :], kg_ref[...], cos[rows, :], sin[rows, :], dkt[:, rows].T * score_scale
            )
            dv = dvt[:, rows].T
            sk_k = sk_k + mm(xt[:, rows], dk.astype(BF16))
            sk_v = sk_v + mm(xt[:, rows], dv.astype(BF16))
            target = (back2_ref, back1_ref, own_ref)[part]
            target[:, k_lanes] = dk.astype(target.dtype)
            target[:, v_lanes] = dv.astype(target.dtype)
        sk_ref[:, :, pl.ds(pl.multiple_of(head * 2 * HD, 2 * HD), 2 * HD)] = skq[...].astype(BF16).reshape(64, 2, -1)
        sk_ref[:, :, pl.ds(pl.multiple_of(head * HD + 4 * HD, HD), HD)] = sk_k.astype(BF16).reshape(64, 2, -1)
        sk_ref[:, :, pl.ds(pl.multiple_of(head * HD + 6 * HD, HD), HD)] = sk_v.astype(BF16).reshape(64, 2, -1)
        sk_ref[:, :, pl.ds(pl.multiple_of(head * 2 * HD + 8 * HD, 2 * HD), 2 * HD)] = sko[...].astype(BF16).reshape(64, 2, -1)


def attention(shard, q_raw, d_out, k_raw, values, kv1, kv2, sketches, q_gain, k_gain, tables):
    arrays = [q_raw, d_out, k_raw, values, kv1, kv2, *sketches, q_gain[None, :], k_gain[None, :]] + tables
    return pl.pallas_call(
        attention_kernel,
        in_specs=[pl.BlockSpec(memory_space=pltpu.SMEM)] + [pl.BlockSpec(memory_space=pl.ANY)] * N_IN,
        out_specs=[pl.BlockSpec(memory_space=pl.ANY)] * 5,
        out_shape=[
            jax.ShapeDtypeStruct((TOK, 4 * HD), BF16),
            jax.ShapeDtypeStruct((TOK, 4 * HD), F32),
            jax.ShapeDtypeStruct((TOK, 4 * HD), BF16),
            jax.ShapeDtypeStruct((TOK, 4 * HD), BF16),
            jax.ShapeDtypeStruct((64, 2, 12 * HD), BF16),
        ],
        scratch_shapes=[pltpu.VMEM(a.shape, a.dtype) for a in arrays[:N_IN]] + [
            pltpu.VMEM((TOK, 4 * HD), BF16),
            pltpu.VMEM((TOK, 4 * HD), F32),
            pltpu.VMEM((TOK, 4 * HD), BF16),
            pltpu.VMEM((TOK, 4 * HD), BF16),
            pltpu.VMEM((64, 2, 12 * HD), BF16),
            pltpu.VMEM((SPAN, HD), BF16),
            pltpu.VMEM((SPAN, HD), BF16),
            pltpu.VMEM((SPAN, HD), F32),
            pltpu.VMEM((SPAN, HD), F32),
            pltpu.VMEM((SPAN, HD), F32),
            pltpu.VMEM((2 * QT, NBLK * KB), F32),
            pltpu.VMEM((2 * QT, NBLK * KB), F32),
            pltpu.VMEM((HD, SPAN), F32),
            pltpu.VMEM((HD, SPAN), F32),
            pltpu.VMEM((HD, SPAN), BF16),
            pltpu.VMEM((HD, TOK), BF16),
            pltpu.VMEM((HD, 2 * HD), F32),
            pltpu.VMEM((HD, 2 * HD), F32),
            pltpu.SemaphoreType.DMA((N_IN,)),
            pltpu.SemaphoreType.DMA((2, 8)),
        ],
        compiler_params=pltpu.CompilerParams(vmem_limit_bytes=ATTN_VMEM),
        cost_estimate=pl.CostEstimate(
            flops=6 * 4 * 2 * TOK * SPAN * HD, bytes_accessed=6 << 20, transcendentals=4 * TOK * SPAN
        ),
    )(shard, *arrays)


def shift(x, by):
    count = lax.axis_size("seq")
    pairs = [(i, i + by) for i in range(count) if 0 <= i + by < count]
    return lax.ppermute(x, "seq", pairs)


def swap(x, bit):
    count = lax.axis_size("head")
    return lax.ppermute(x, "head", [(i, i ^ bit) for i in range(count)])


def z_swap(x, turn):
    count = lax.axis_size("head")
    return lax.ppermute(x, "head", [(i, i ^ (2, 6)[(i + turn) % 2]) for i in range(count)])


def pair_swap(x):
    count = lax.axis_size("seq")
    return lax.ppermute(x, "seq", [(i, i ^ 1) for i in range(count)])


def one_turn(step, start):
    return lax.fori_loop(0, lax.optimization_barrier(jnp.int32(1)), lambda i, carry: step(), start)


def per_device(
    layer_input, omega_in, upstream, omega_out, q_raw, k_raw, values, d_out, q_gain, k_gain
):
    kv = jnp.concatenate([k_raw, values], axis=1)
    kv, layer_input, upstream = lax.optimization_barrier((kv, layer_input, upstream))
    odd = lax.axis_index("seq") % 2 == 1
    first = lax.axis_index("head") % 2 == 0
    kv2 = shift(kv, 2)
    partial_x = jnp.dot(layer_input, omega_in, preferred_element_type=F32)
    partial_y = jnp.dot(upstream, omega_out, preferred_element_type=F32)

    keep = jnp.where(first, partial_x, partial_y)
    give = jnp.where(first, partial_y, partial_x).astype(BF16)

    def sum_near():
        total = keep + swap(give, 1).astype(F32)
        return (total + z_swap(total.astype(BF16), 0).astype(F32)).astype(BF16)

    half = one_turn(sum_near, keep.astype(BF16))
    kv1 = pair_swap(jnp.where(odd, kv2, kv))
    mine = (half.astype(F32) + z_swap(half, 1).astype(F32)).astype(BF16)
    other = swap(mine, 1)
    x0, y0 = jnp.where(first, mine, other), jnp.where(first, other, mine)
    x1 = shift(x0, 1)
    x2 = shift(x0, 2)
    shard = lax.axis_index("seq").astype(jnp.int32)[None]
    tables = [jnp.asarray(t) for t in rope_tables(lax.axis_size("seq"))]
    query_grad, own, back1, back2, sketches = attention(
        shard, q_raw, d_out, k_raw, values, kv1, kv2, (x0, x1, x2, y0), q_gain, k_gain, tables
    )
    near = pair_swap(back1).astype(F32)
    back2 = back2.astype(F32)
    far = shift(jnp.where(odd, back2 + near, back2).astype(BF16), -2)
    pieces = lax.all_to_all(sketches, "seq", 0, 0, tiled=True)
    total = jnp.sum(pieces.astype(F32), axis=0)
    q_cols, kv_cols = 4 * HD, 2 * HD

    def finish(begin):
        cols = slice(begin, begin + kv_cols)
        return (own[:, cols] + jnp.where(odd, 0.0, near[:, cols]) + far[:, cols].astype(F32)).astype(BF16)

    return (
        query_grad,
        finish(0),
        finish(kv_cols),
        total[:, :q_cols],
        total[:, q_cols : q_cols + kv_cols],
        total[:, q_cols + kv_cols : q_cols + 2 * kv_cols],
        total[:, q_cols + 2 * kv_cols :],
    )


def solution(mesh):
    split = P("seq", "head")
    in_specs = (split, P("head", None), split, P("head", None), split, split, split, split, P(), P())
    return jax.shard_map(
        per_device, mesh=mesh, in_specs=in_specs, out_specs=(split,) * 7, check_vma=False
    )
```

```python
import jax
import jax.numpy as jnp
import numpy as np
from jax import lax
from jax.experimental import pallas as pl
from jax.experimental.pallas import tpu as pltpu
from jax.sharding import PartitionSpec as P

WINDOW = 1024
HD = 128
TOK = 512
QT = 256
KB = 256
GROUP = 64
ATTN_VMEM = 60 << 20
SPAN = 1536
NBLK = 5
score_scale = 168.0 ** (-0.5)
LOG2E = 1.4426950408889634
epsilon = 1e-06
rope_base = 10000.0
F32 = jnp.float32
BF16 = jnp.bfloat16


def rope_tables(shards):
    freq = rope_base ** (-(np.arange(64, dtype=np.float64) * 2.0 / HD))
    freq = np.concatenate([freq, freq])[None, :]
    starts = (np.arange(-2, shards + 6) * TOK, np.arange(TOK // GROUP) * GROUP, np.arange(GROUP))
    angles = [at.astype(np.float64)[:, None] * freq for at in starts]
    return [f(a).astype(np.float32) for a in angles for f in (np.cos, np.sin)]


def lane_mean(x):
    high = x.astype(BF16)
    low = (x - high.astype(F32)).astype(BF16)
    ones = jnp.full((HD, HD), 1.0 / HD, BF16)
    return mm(high, ones) + mm(low, ones)


def norm_scale(raw):
    return lax.rsqrt(lane_mean(raw * raw) + epsilon)


def rope_forward(normed, cos, sin_signed):
    return normed * cos + pltpu.roll(normed, 64, 1) * sin_signed


def prep_back(raw, r, gain, cos, sin_signed, grad):
    d_norm = (grad * cos - pltpu.roll(grad, 64, 1) * sin_signed) * gain
    return r * d_norm - raw * ((r * r * r) * lane_mean(raw * d_norm))


def mult(a, n):
    return a if isinstance(a, int) else pl.multiple_of(a, n)


def mm(a, b):
    return lax.dot_general(a, b, (((1,), (0,)), ((), ())), preferred_element_type=F32)


def mm_t(a, b):
    return lax.dot_general(a, b, (((1,), (1,)), ((), ())), preferred_element_type=F32)


N_IN = 18


def attention_kernel(
    shard_ref, q_hbm, do_hbm, k0_hbm, v0_hbm, kv1_hbm, kv2_hbm, x0_hbm, x1_hbm, x2_hbm, y_hbm,
    qg_hbm, kg_hbm, cb_hbm, sb_hbm, cm_hbm, sm_hbm, cl_hbm, sl_hbm,
    qgrad_hbm, own_hbm, back1_hbm, back2_hbm, sk_hbm,
    q_ref, do_ref, k0_ref, v0_ref, kv1_ref, kv2_ref, x0_ref, x1_ref, x2_ref, y_ref,
    qg_ref, kg_ref, cb_ref, sb_ref, cm_ref, sm_ref, cl_ref, sl_ref,
    qgrad_ref, own_ref, back1_ref, back2_ref, sk_ref,
    kp, vx, r_k, cos, sin, e_sc, dp_sc, dkt, dvt, xt, yt, skq, sko, in_sems, out_sems,
):
    sources = (cb_hbm, sb_hbm, cm_hbm, sm_hbm, cl_hbm, sl_hbm, qg_hbm, kg_hbm) + (k0_hbm, kv2_hbm, kv1_hbm, v0_hbm, q_hbm, do_hbm, x0_hbm, x1_hbm, x2_hbm, y_hbm)
    targets = (cb_ref, sb_ref, cm_ref, sm_ref, cl_ref, sl_ref, qg_ref, kg_ref) + (k0_ref, kv2_ref, kv1_ref, v0_ref, q_ref, do_ref, x0_ref, x1_ref, x2_ref, y_ref)
    loads = [pltpu.make_async_copy(a, b, in_sems.at[n]) for n, (a, b) in enumerate(zip(sources, targets))]
    for load in loads:
        load.start()
    shard = shard_ref[0]
    for load in loads[:8]:
        load.wait()
    lane = lax.broadcasted_iota(jnp.int32, (1, HD), 1)
    sign = jnp.where(lane < HD // 2, -1.0, 1.0)
    for part in range(3):
        cb = cb_ref[pl.ds(shard + part, 1), :]
        sb = sb_ref[pl.ds(shard + part, 1), :]
        for group in range(TOK // GROUP):
            cm = cm_ref[group : group + 1, :]
            sm = sm_ref[group : group + 1, :]
            c = cb * cm - sb * sm
            s = sb * cm + cb * sm
            rows = slice(part * TOK + group * GROUP, part * TOK + (group + 1) * GROUP)
            cos[rows, :] = c * cl_ref[...] - s * sl_ref[...]
            sin[rows, :] = (s * cl_ref[...] + c * sl_ref[...]) * sign
    for load in loads[8:12]:
        load.wait()

    def wait_queries():
        for load in loads[12:14]:
            load.wait()

    def wait_sketches():
        for load in loads[14:]:
            load.wait()
        for part, x_ref in enumerate((x2_ref, x1_ref, x0_ref)):
            xt[:, part * TOK : (part + 1) * TOK] = x_ref[...].T
        yt[...] = y_ref[...].T

    refs = (
        shard, q_ref, do_ref, k0_ref, v0_ref, kv1_ref, kv2_ref, qg_ref, kg_ref,
        qgrad_ref, own_ref, back1_ref, back2_ref, sk_ref,
        kp, vx, r_k, cos, sin, e_sc, dp_sc, dkt, dvt, xt, yt, skq, sko,
    )

    def stores(head):
        lanes = pl.ds(mult(head * 2 * HD, 2 * HD), 2 * HD)
        out = [(qgrad_ref.at[:, lanes], qgrad_hbm.at[:, lanes])]
        for kind in range(2):
            lanes = pl.ds(mult(head * HD + kind * 2 * HD, HD), HD)
            for a, b in ((own_ref, own_hbm), (back1_ref, back1_hbm), (back2_ref, back2_hbm)):
                out.append((a.at[:, lanes], b.at[:, lanes]))
        return [pltpu.make_async_copy(a, b, out_sems.at[head, n]) for n, (a, b) in enumerate(out)]

    for head in range(2):
        for tile in range(2):
            attention_step(head, tile, wait_queries, wait_sketches, *refs)
        for store in stores(head):
            store.start()

    sketch_store = pltpu.make_async_copy(sk_ref, sk_hbm, out_sems.at[0, 7])
    sketch_store.start()
    for head in range(2):
        for store in stores(head):
            store.wait()
    sketch_store.wait()


def attention_step(
    head, tile, wait_queries, wait_sketches, shard, q_ref, do_ref, k0_ref, v0_ref, kv1_ref, kv2_ref, qg_ref, kg_ref,
    qgrad_ref, own_ref, back1_ref, back2_ref, sk_ref,
    kp, vx, r_k, cos, sin, e_sc, dp_sc, dkt, dvt, xt, yt, skq, sko,
):
    k_lanes = pl.ds(mult(head * HD, HD), HD)
    v_lanes = pl.ds(mult(head * HD + 2 * HD, HD), HD)
    k_parts = (kv2_ref.at[:, k_lanes], kv1_ref.at[:, k_lanes], k0_ref.at[:, k_lanes])
    v_parts = (kv2_ref.at[:, v_lanes], kv1_ref.at[:, v_lanes], v0_ref.at[:, k_lanes])

    if tile == 0:
        skq[...] = jnp.zeros_like(skq)
        sko[...] = jnp.zeros_like(sko)
        for part, (k_ref, v_ref) in enumerate(zip(k_parts, v_parts)):
            rows = slice(part * TOK, (part + 1) * TOK)
            raw = k_ref[...].astype(F32)
            r = norm_scale(raw)
            r_k[rows, :] = r
            normed = raw * r * kg_ref[...]
            kp[rows, :] = rope_forward(normed, cos[rows, :], sin[rows, :]).astype(BF16)
            vx[rows, :] = v_ref[...]
        dkt[...] = jnp.zeros_like(dkt)
        dvt[...] = jnp.zeros_like(dvt)

    if head == 0 and tile == 0:
        wait_queries()
    tile_rows = pl.ds(mult(tile * QT, QT), QT)
    q_rows = pl.ds(mult(2 * TOK + tile * QT, QT), QT)
    q_lanes = [pl.ds(mult(head * 2 * HD + g * HD, HD), HD) for g in range(2)]
    cos_q = cos[q_rows, :]
    sin_q = sin[q_rows, :]
    q_parts = []
    r_parts = []
    for lanes in q_lanes:
        raw = q_ref[tile_rows, lanes].astype(F32)
        r_parts.append(norm_scale(raw))
        q_parts.append(rope_forward(raw * r_parts[-1] * qg_ref[...], cos_q, sin_q))
    q = jnp.concatenate(q_parts, axis=0)
    d_out = jnp.concatenate([do_ref[tile_rows, lanes] for lanes in q_lanes], axis=0)
    q_low = q.astype(BF16)
    q_t = q_low.T
    do_t = d_out.T

    rows_i = lax.broadcasted_iota(jnp.int32, (2 * QT, KB), 0) & (QT - 1)
    cols_i = lax.broadcasted_iota(jnp.int32, (2 * QT, KB), 1)

    l_acc = jnp.zeros((2 * QT, HD), F32)
    u_acc = jnp.zeros((2 * QT, HD), F32)
    for b in range(NBLK):
        at = pl.ds(mult(tile * QT + b * KB, KB), KB)
        cols = slice(b * KB, (b + 1) * KB)
        s = mm_t(q_low, kp[at, :])
        e = jnp.exp2(s * (score_scale * LOG2E))
        key_shard = shard - 2 + (tile * QT + b * KB) // TOK
        if b == 0:
            e = jnp.where((cols_i > rows_i) & (key_shard >= 0), e, 0.0)
        elif b == NBLK - 1:
            e = jnp.where(cols_i <= rows_i, e, 0.0)
        else:
            e = e * jnp.where(key_shard >= 0, 1.0, 0.0)
        dp = mm_t(d_out, vx[at, :])
        ed = e * dp
        l_acc = l_acc + e[:, :HD] + e[:, HD:]
        u_acc = u_acc + ed[:, :HD] + ed[:, HD:]
        e_sc[:, cols] = e
        dp_sc[:, cols] = dp
    inv = 1.0 / jnp.sum(l_acc, axis=-1, keepdims=True)
    delta = jnp.sum(u_acc, axis=-1, keepdims=True) * inv

    out = jnp.zeros((2 * QT, HD), F32)
    dq = jnp.zeros((2 * QT, HD), F32)
    for b in range(NBLK):
        at = pl.ds(mult(tile * QT + b * KB, KB), KB)
        cols = slice(b * KB, (b + 1) * KB)
        p = e_sc[:, cols] * inv
        ds = (p * (dp_sc[:, cols] - delta)).astype(BF16)
        p = p.astype(BF16)
        out = out + mm(p, vx[at, :])
        dq = dq + mm(ds, kp[at, :])
        dvt[:, at] += mm(do_t, p)
        dkt[:, at] += mm(q_t, ds)
    if head == 0 and tile == 0:
        wait_sketches()
    x_tile = xt[:, q_rows]
    y_tile = yt[:, tile_rows]
    for g in range(2):
        rows = slice(g * QT, (g + 1) * QT)
        lanes = slice(g * HD, (g + 1) * HD)
        raw = q_ref[tile_rows, q_lanes[g]].astype(F32)
        q_grad = prep_back(raw, r_parts[g], qg_ref[...], cos_q, sin_q, dq[rows] * score_scale).astype(BF16)
        qgrad_ref[tile_rows, q_lanes[g]] = q_grad
        skq[:, lanes] += mm(x_tile, q_grad)
        sko[:, lanes] += mm(y_tile, out[rows].astype(BF16))

    if tile == 1:
        sk_k = jnp.zeros((HD, HD), F32)
        sk_v = jnp.zeros((HD, HD), F32)
        for part, k_ref in enumerate(k_parts):
            rows = slice(part * TOK, (part + 1) * TOK)
            raw = k_ref[...].astype(F32)
            dk = prep_back(
                raw, r_k[rows, :], kg_ref[...], cos[rows, :], sin[rows, :], dkt[:, rows].T * score_scale
            )
            dv = dvt[:, rows].T
            sk_k = sk_k + mm(xt[:, rows], dk.astype(BF16))
            sk_v = sk_v + mm(xt[:, rows], dv.astype(BF16))
            target = (back2_ref, back1_ref, own_ref)[part]
            target[:, k_lanes] = dk.astype(target.dtype)
            target[:, v_lanes] = dv.astype(target.dtype)
        sk_ref[:, :, pl.ds(mult(head * 2 * HD, 2 * HD), 2 * HD)] = skq[...].astype(BF16).reshape(64, 2, -1)
        sk_ref[:, :, pl.ds(mult(head * HD + 4 * HD, HD), HD)] = sk_k.astype(BF16).reshape(64, 2, -1)
        sk_ref[:, :, pl.ds(mult(head * HD + 6 * HD, HD), HD)] = sk_v.astype(BF16).reshape(64, 2, -1)
        sk_ref[:, :, pl.ds(mult(head * 2 * HD + 8 * HD, 2 * HD), 2 * HD)] = sko[...].astype(BF16).reshape(64, 2, -1)


def attention(shard, q_raw, d_out, k_raw, values, kv1, kv2, sketches, q_gain, k_gain, tables):
    arrays = [q_raw, d_out, k_raw, values, kv1, kv2, *sketches, q_gain[None, :], k_gain[None, :]] + tables
    return pl.pallas_call(
        attention_kernel,
        in_specs=[pl.BlockSpec(memory_space=pltpu.SMEM)] + [pl.BlockSpec(memory_space=pl.ANY)] * N_IN,
        out_specs=[pl.BlockSpec(memory_space=pl.ANY)] * 5,
        out_shape=[
            jax.ShapeDtypeStruct((TOK, 4 * HD), BF16),
            jax.ShapeDtypeStruct((TOK, 4 * HD), BF16),
            jax.ShapeDtypeStruct((TOK, 4 * HD), BF16),
            jax.ShapeDtypeStruct((TOK, 4 * HD), BF16),
            jax.ShapeDtypeStruct((64, 2, 12 * HD), BF16),
        ],
        scratch_shapes=[pltpu.VMEM(a.shape, a.dtype) for a in arrays[:N_IN]] + [
            pltpu.VMEM((TOK, 4 * HD), BF16),
            pltpu.VMEM((TOK, 4 * HD), BF16),
            pltpu.VMEM((TOK, 4 * HD), BF16),
            pltpu.VMEM((TOK, 4 * HD), BF16),
            pltpu.VMEM((64, 2, 12 * HD), BF16),
            pltpu.VMEM((SPAN, HD), BF16),
            pltpu.VMEM((SPAN, HD), BF16),
            pltpu.VMEM((SPAN, HD), F32),
            pltpu.VMEM((SPAN, HD), F32),
            pltpu.VMEM((SPAN, HD), F32),
            pltpu.VMEM((2 * QT, NBLK * KB), F32),
            pltpu.VMEM((2 * QT, NBLK * KB), F32),
            pltpu.VMEM((HD, SPAN), F32),
            pltpu.VMEM((HD, SPAN), F32),
            pltpu.VMEM((HD, SPAN), BF16),
            pltpu.VMEM((HD, TOK), BF16),
            pltpu.VMEM((HD, 2 * HD), F32),
            pltpu.VMEM((HD, 2 * HD), F32),
            pltpu.SemaphoreType.DMA((N_IN,)),
            pltpu.SemaphoreType.DMA((2, 8)),
        ],
        compiler_params=pltpu.CompilerParams(vmem_limit_bytes=ATTN_VMEM),
        cost_estimate=pl.CostEstimate(
            flops=6 * 4 * 2 * TOK * SPAN * HD, bytes_accessed=6 << 20, transcendentals=4 * TOK * SPAN
        ),
    )(shard, *arrays)


def shift(x, by):
    count = lax.axis_size("seq")
    pairs = [(i, i + by) for i in range(count) if 0 <= i + by < count]
    return lax.ppermute(x, "seq", pairs)


def swap(x, bit):
    count = lax.axis_size("head")
    return lax.ppermute(x, "head", [(i, i ^ bit) for i in range(count)])


def z_swap(x, turn):
    count = lax.axis_size("head")
    return lax.ppermute(x, "head", [(i, i ^ (2, 6)[(i + turn) % 2]) for i in range(count)])


def pair_swap(x):
    count = lax.axis_size("seq")
    return lax.ppermute(x, "seq", [(i, i ^ 1) for i in range(count)])


def one_turn(step, start):
    return lax.fori_loop(0, lax.optimization_barrier(jnp.int32(1)), lambda i, carry: step(carry), start)


def per_device(
    layer_input, omega_in, upstream, omega_out, q_raw, k_raw, values, d_out, q_gain, k_gain
):
    kv = jnp.concatenate([k_raw, values], axis=1)
    kv, layer_input, upstream = lax.optimization_barrier((kv, layer_input, upstream))
    odd = lax.axis_index("seq") % 2 == 1
    first = lax.axis_index("head") % 2 == 0
    kv2 = shift(kv, 2)
    partial_x = jnp.dot(layer_input, omega_in, preferred_element_type=F32)
    partial_y = jnp.dot(upstream, omega_out, preferred_element_type=F32)


    def sum_near():
        got = swap(jnp.where(first, partial_y, partial_x).astype(BF16), 1)
        total = jnp.where(first, partial_x, partial_y) + got.astype(F32)
        return (total + z_swap(total.astype(BF16), 0).astype(F32)).astype(BF16)

    def sum_far(half):
        return (half.astype(F32) + z_swap(half, 1).astype(F32)).astype(BF16)

    half = one_turn(lambda carry: sum_near(), partial_x.astype(BF16))
    kv1 = pair_swap(jnp.where(odd, kv2, kv))
    mine = one_turn(sum_far, half)
    other = swap(mine, 1)
    x0, y0 = jnp.where(first, mine, other), jnp.where(first, other, mine)
    x1 = shift(x0, 1)
    x2 = shift(x0, 2)
    shard = lax.axis_index("seq").astype(jnp.int32)[None]
    tables = [jnp.asarray(t) for t in rope_tables(lax.axis_size("seq"))]
    query_grad, own, back1, back2, sketches = attention(
        shard, q_raw, d_out, k_raw, values, kv1, kv2, (x0, x1, x2, y0), q_gain, k_gain, tables
    )
    near = pair_swap(back1).astype(F32)
    back2 = back2.astype(F32)
    far = shift(jnp.where(odd, back2 + near, back2).astype(BF16), -2)
    pieces = lax.all_to_all(sketches, "seq", 0, 0, tiled=True)
    total = jnp.sum(pieces.astype(F32), axis=0)
    q_cols, kv_cols = 4 * HD, 2 * HD

    kv_grad = (own.astype(F32) + jnp.where(odd, 0.0, near) + far.astype(F32)).astype(BF16)
    return (
        query_grad,
        kv_grad[:, :kv_cols],
        kv_grad[:, kv_cols:],
        total[:, :q_cols],
        total[:, q_cols : q_cols + kv_cols],
        total[:, q_cols + kv_cols : q_cols + 2 * kv_cols],
        total[:, q_cols + 2 * kv_cols :],
    )


def solution(mesh):
    split = P("seq", "head")
    in_specs = (split, P("head", None), split, P("head", None), split, split, split, split, P(), P())
    return jax.shard_map(
        per_device, mesh=mesh, in_specs=in_specs, out_specs=(split,) * 7, check_vma=False
    )
```

```python
import jax
import jax.numpy as jnp
import numpy as np
from jax import lax
from jax.experimental import pallas as pl
from jax.experimental.pallas import tpu as pltpu
from jax.sharding import PartitionSpec as P

WINDOW = 1024
HD = 128
TOK = 512
QT = 256
KB = 256
GROUP = 64
ATTN_VMEM = 60 << 20
SPAN = 1536
NBLK = 5
score_scale = 168.0 ** (-0.5)
LOG2E = 1.4426950408889634
epsilon = 1e-06
rope_base = 10000.0
F32 = jnp.float32
BF16 = jnp.bfloat16


def rope_tables(shards):
    freq = rope_base ** (-(np.arange(64, dtype=np.float64) * 2.0 / HD))
    freq = np.concatenate([freq, freq])[None, :]
    starts = (np.arange(-2, shards + 6) * TOK, np.arange(TOK // GROUP) * GROUP, np.arange(GROUP))
    angles = [at.astype(np.float64)[:, None] * freq for at in starts]
    return [f(a).astype(np.float32) for a in angles for f in (np.cos, np.sin)]


def lane_mean(x):
    high = x.astype(BF16)
    low = (x - high.astype(F32)).astype(BF16)
    ones = jnp.full((HD, HD), 1.0 / HD, BF16)
    return mm(high, ones) + mm(low, ones)


def norm_scale(raw):
    return lax.rsqrt(lane_mean(raw * raw) + epsilon)


def rope_forward(normed, cos, sin_signed):
    return normed * cos + pltpu.roll(normed, 64, 1) * sin_signed


def prep_back(raw, r, gain, cos, sin_signed, grad):
    d_norm = (grad * cos - pltpu.roll(grad, 64, 1) * sin_signed) * gain
    return r * d_norm - raw * ((r * r * r) * lane_mean(raw * d_norm))


def mult(a, n):
    return a if isinstance(a, int) else pl.multiple_of(a, n)


def mm(a, b):
    return lax.dot_general(a, b, (((1,), (0,)), ((), ())), preferred_element_type=F32)


def mm_t(a, b):
    return lax.dot_general(a, b, (((1,), (1,)), ((), ())), preferred_element_type=F32)


N_IN = 18


def attention_kernel(
    shard_ref, q_hbm, do_hbm, k0_hbm, v0_hbm, kv1_hbm, kv2_hbm, x0_hbm, x1_hbm, x2_hbm, y_hbm,
    qg_hbm, kg_hbm, cb_hbm, sb_hbm, cm_hbm, sm_hbm, cl_hbm, sl_hbm,
    qgrad_hbm, own_hbm, back1_hbm, back2_hbm, sk_hbm,
    q_ref, do_ref, k0_ref, v0_ref, kv1_ref, kv2_ref, x0_ref, x1_ref, x2_ref, y_ref,
    qg_ref, kg_ref, cb_ref, sb_ref, cm_ref, sm_ref, cl_ref, sl_ref,
    qgrad_ref, own_ref, back1_ref, back2_ref, sk_ref,
    kp, vx, r_k, cos, sin, e_sc, dp_sc, dkt, dvt, xt, yt, skq, sko, in_sems, out_sems,
):
    sources = (cb_hbm, sb_hbm, cm_hbm, sm_hbm, cl_hbm, sl_hbm, qg_hbm, kg_hbm) + (k0_hbm, kv2_hbm, kv1_hbm, v0_hbm, q_hbm, do_hbm, x0_hbm, x1_hbm, x2_hbm, y_hbm)
    targets = (cb_ref, sb_ref, cm_ref, sm_ref, cl_ref, sl_ref, qg_ref, kg_ref) + (k0_ref, kv2_ref, kv1_ref, v0_ref, q_ref, do_ref, x0_ref, x1_ref, x2_ref, y_ref)
    loads = [pltpu.make_async_copy(a, b, in_sems.at[n]) for n, (a, b) in enumerate(zip(sources, targets))]
    for load in loads:
        load.start()
    shard = shard_ref[0]
    for load in loads[:8]:
        load.wait()
    lane = lax.broadcasted_iota(jnp.int32, (1, HD), 1)
    sign = jnp.where(lane < HD // 2, -1.0, 1.0)
    for part in range(3):
        cb = cb_ref[pl.ds(shard + part, 1), :]
        sb = sb_ref[pl.ds(shard + part, 1), :]
        for group in range(TOK // GROUP):
            cm = cm_ref[group : group + 1, :]
            sm = sm_ref[group : group + 1, :]
            c = cb * cm - sb * sm
            s = sb * cm + cb * sm
            rows = slice(part * TOK + group * GROUP, part * TOK + (group + 1) * GROUP)
            cos[rows, :] = c * cl_ref[...] - s * sl_ref[...]
            sin[rows, :] = (s * cl_ref[...] + c * sl_ref[...]) * sign
    for load in loads[8:12]:
        load.wait()

    def wait_queries():
        for load in loads[12:14]:
            load.wait()

    def wait_sketches():
        for load in loads[14:]:
            load.wait()
        for part, x_ref in enumerate((x2_ref, x1_ref, x0_ref)):
            xt[:, part * TOK : (part + 1) * TOK] = x_ref[...].T
        yt[...] = y_ref[...].T

    refs = (
        shard, q_ref, do_ref, k0_ref, v0_ref, kv1_ref, kv2_ref, qg_ref, kg_ref,
        qgrad_ref, own_ref, back1_ref, back2_ref, sk_ref,
        kp, vx, r_k, cos, sin, e_sc, dp_sc, dkt, dvt, xt, yt, skq, sko,
    )

    def stores(head):
        lanes = pl.ds(mult(head * 2 * HD, 2 * HD), 2 * HD)
        out = [(qgrad_ref.at[:, lanes], qgrad_hbm.at[:, lanes])]
        for kind in range(2):
            lanes = pl.ds(mult(head * HD + kind * 2 * HD, HD), HD)
            for a, b in ((own_ref, own_hbm), (back1_ref, back1_hbm), (back2_ref, back2_hbm)):
                out.append((a.at[:, lanes], b.at[:, lanes]))
        return [pltpu.make_async_copy(a, b, out_sems.at[head, n]) for n, (a, b) in enumerate(out)]

    for head in range(2):
        for tile in range(2):
            attention_step(head, tile, wait_queries, wait_sketches, *refs)
        for store in stores(head):
            store.start()

    sketch_store = pltpu.make_async_copy(sk_ref, sk_hbm, out_sems.at[0, 7])
    sketch_store.start()
    for head in range(2):
        for store in stores(head):
            store.wait()
    sketch_store.wait()


def attention_step(
    head, tile, wait_queries, wait_sketches, shard, q_ref, do_ref, k0_ref, v0_ref, kv1_ref, kv2_ref, qg_ref, kg_ref,
    qgrad_ref, own_ref, back1_ref, back2_ref, sk_ref,
    kp, vx, r_k, cos, sin, e_sc, dp_sc, dkt, dvt, xt, yt, skq, sko,
):
    k_lanes = pl.ds(mult(head * HD, HD), HD)
    v_lanes = pl.ds(mult(head * HD + 2 * HD, HD), HD)
    k_parts = (kv2_ref.at[:, k_lanes], kv1_ref.at[:, k_lanes], k0_ref.at[:, k_lanes])
    v_parts = (kv2_ref.at[:, v_lanes], kv1_ref.at[:, v_lanes], v0_ref.at[:, k_lanes])

    if tile == 0:
        skq[...] = jnp.zeros_like(skq)
        sko[...] = jnp.zeros_like(sko)
        for part, (k_ref, v_ref) in enumerate(zip(k_parts, v_parts)):
            rows = slice(part * TOK, (part + 1) * TOK)
            raw = k_ref[...].astype(F32)
            r = norm_scale(raw)
            r_k[rows, :] = r
            normed = raw * r * kg_ref[...]
            kp[rows, :] = rope_forward(normed, cos[rows, :], sin[rows, :]).astype(BF16)
            vx[rows, :] = v_ref[...]
        dkt[...] = jnp.zeros_like(dkt)
        dvt[...] = jnp.zeros_like(dvt)

    if head == 0 and tile == 0:
        wait_queries()
    tile_rows = pl.ds(mult(tile * QT, QT), QT)
    q_rows = pl.ds(mult(2 * TOK + tile * QT, QT), QT)
    q_lanes = [pl.ds(mult(head * 2 * HD + g * HD, HD), HD) for g in range(2)]
    cos_q = cos[q_rows, :]
    sin_q = sin[q_rows, :]
    q_parts = []
    r_parts = []
    for lanes in q_lanes:
        raw = q_ref[tile_rows, lanes].astype(F32)
        r_parts.append(norm_scale(raw))
        q_parts.append(rope_forward(raw * r_parts[-1] * qg_ref[...], cos_q, sin_q))
    q = jnp.concatenate(q_parts, axis=0)
    d_out = jnp.concatenate([do_ref[tile_rows, lanes] for lanes in q_lanes], axis=0)
    q_low = q.astype(BF16)
    q_t = q_low.T
    do_t = d_out.T

    rows_i = lax.broadcasted_iota(jnp.int32, (2 * QT, KB), 0) & (QT - 1)
    cols_i = lax.broadcasted_iota(jnp.int32, (2 * QT, KB), 1)

    l_acc = jnp.zeros((2 * QT, HD), F32)
    u_acc = jnp.zeros((2 * QT, HD), F32)
    for b in range(NBLK):
        at = pl.ds(mult(tile * QT + b * KB, KB), KB)
        cols = slice(b * KB, (b + 1) * KB)
        s = mm_t(q_low, kp[at, :])
        e = jnp.exp2(s * (score_scale * LOG2E))
        key_shard = shard - 2 + (tile * QT + b * KB) // TOK
        if b == 0:
            e = jnp.where((cols_i > rows_i) & (key_shard >= 0), e, 0.0)
        elif b == NBLK - 1:
            e = jnp.where(cols_i <= rows_i, e, 0.0)
        else:
            e = e * jnp.where(key_shard >= 0, 1.0, 0.0)
        dp = mm_t(d_out, vx[at, :])
        ed = e * dp
        l_acc = l_acc + e[:, :HD] + e[:, HD:]
        u_acc = u_acc + ed[:, :HD] + ed[:, HD:]
        e_sc[:, cols] = e
        dp_sc[:, cols] = dp
    inv = 1.0 / jnp.sum(l_acc, axis=-1, keepdims=True)
    delta = jnp.sum(u_acc, axis=-1, keepdims=True) * inv

    out = jnp.zeros((2 * QT, HD), F32)
    dq = jnp.zeros((2 * QT, HD), F32)
    for b in range(NBLK):
        at = pl.ds(mult(tile * QT + b * KB, KB), KB)
        cols = slice(b * KB, (b + 1) * KB)
        p = e_sc[:, cols] * inv
        ds = (p * (dp_sc[:, cols] - delta)).astype(BF16)
        p = p.astype(BF16)
        out = out + mm(p, vx[at, :])
        dq = dq + mm(ds, kp[at, :])
        dvt[:, at] += mm(do_t, p)
        dkt[:, at] += mm(q_t, ds)
    if head == 0 and tile == 0:
        wait_sketches()
    x_tile = xt[:, q_rows]
    y_tile = yt[:, tile_rows]
    for g in range(2):
        rows = slice(g * QT, (g + 1) * QT)
        lanes = slice(g * HD, (g + 1) * HD)
        raw = q_ref[tile_rows, q_lanes[g]].astype(F32)
        q_grad = prep_back(raw, r_parts[g], qg_ref[...], cos_q, sin_q, dq[rows] * score_scale).astype(BF16)
        qgrad_ref[tile_rows, q_lanes[g]] = q_grad
        skq[:, lanes] += mm(x_tile, q_grad)
        sko[:, lanes] += mm(y_tile, out[rows].astype(BF16))

    if tile == 1:
        sk_k = jnp.zeros((HD, HD), F32)
        sk_v = jnp.zeros((HD, HD), F32)
        for part, k_ref in enumerate(k_parts):
            rows = slice(part * TOK, (part + 1) * TOK)
            raw = k_ref[...].astype(F32)
            dk = prep_back(
                raw, r_k[rows, :], kg_ref[...], cos[rows, :], sin[rows, :], dkt[:, rows].T * score_scale
            )
            dv = dvt[:, rows].T
            sk_k = sk_k + mm(xt[:, rows], dk.astype(BF16))
            sk_v = sk_v + mm(xt[:, rows], dv.astype(BF16))
            target = (back2_ref, back1_ref, own_ref)[part]
            target[:, k_lanes] = dk.astype(target.dtype)
            target[:, v_lanes] = dv.astype(target.dtype)
        sk_ref[:, :, pl.ds(mult(head * 2 * HD, 2 * HD), 2 * HD)] = skq[...].astype(BF16).reshape(64, 2, -1)
        sk_ref[:, :, pl.ds(mult(head * HD + 4 * HD, HD), HD)] = sk_k.astype(BF16).reshape(64, 2, -1)
        sk_ref[:, :, pl.ds(mult(head * HD + 6 * HD, HD), HD)] = sk_v.astype(BF16).reshape(64, 2, -1)
        sk_ref[:, :, pl.ds(mult(head * 2 * HD + 8 * HD, 2 * HD), 2 * HD)] = sko[...].astype(BF16).reshape(64, 2, -1)


def attention(shard, q_raw, d_out, k_raw, values, kv1, kv2, sketches, q_gain, k_gain, tables):
    arrays = [q_raw, d_out, k_raw, values, kv1, kv2, *sketches, q_gain[None, :], k_gain[None, :]] + tables
    return pl.pallas_call(
        attention_kernel,
        in_specs=[pl.BlockSpec(memory_space=pltpu.SMEM)] + [pl.BlockSpec(memory_space=pl.ANY)] * N_IN,
        out_specs=[pl.BlockSpec(memory_space=pl.ANY)] * 5,
        out_shape=[
            jax.ShapeDtypeStruct((TOK, 4 * HD), BF16),
            jax.ShapeDtypeStruct((TOK, 4 * HD), BF16),
            jax.ShapeDtypeStruct((TOK, 4 * HD), BF16),
            jax.ShapeDtypeStruct((TOK, 4 * HD), BF16),
            jax.ShapeDtypeStruct((64, 2, 12 * HD), BF16),
        ],
        scratch_shapes=[pltpu.VMEM(a.shape, a.dtype) for a in arrays[:N_IN]] + [
            pltpu.VMEM((TOK, 4 * HD), BF16),
            pltpu.VMEM((TOK, 4 * HD), BF16),
            pltpu.VMEM((TOK, 4 * HD), BF16),
            pltpu.VMEM((TOK, 4 * HD), BF16),
            pltpu.VMEM((64, 2, 12 * HD), BF16),
            pltpu.VMEM((SPAN, HD), BF16),
            pltpu.VMEM((SPAN, HD), BF16),
            pltpu.VMEM((SPAN, HD), F32),
            pltpu.VMEM((SPAN, HD), F32),
            pltpu.VMEM((SPAN, HD), F32),
            pltpu.VMEM((2 * QT, NBLK * KB), F32),
            pltpu.VMEM((2 * QT, NBLK * KB), F32),
            pltpu.VMEM((HD, SPAN), F32),
            pltpu.VMEM((HD, SPAN), F32),
            pltpu.VMEM((HD, SPAN), BF16),
            pltpu.VMEM((HD, TOK), BF16),
            pltpu.VMEM((HD, 2 * HD), F32),
            pltpu.VMEM((HD, 2 * HD), F32),
            pltpu.SemaphoreType.DMA((N_IN,)),
            pltpu.SemaphoreType.DMA((2, 8)),
        ],
        compiler_params=pltpu.CompilerParams(vmem_limit_bytes=ATTN_VMEM),
        cost_estimate=pl.CostEstimate(
            flops=6 * 4 * 2 * TOK * SPAN * HD, bytes_accessed=6 << 20, transcendentals=4 * TOK * SPAN
        ),
    )(shard, *arrays)


def shift(x, by):
    count = lax.axis_size("seq")
    pairs = [(i, i + by) for i in range(count) if 0 <= i + by < count]
    return lax.ppermute(x, "seq", pairs)


def swap(x, bit):
    count = lax.axis_size("head")
    return lax.ppermute(x, "head", [(i, i ^ bit) for i in range(count)])


def z_swap(x, turn):
    count = lax.axis_size("head")
    return lax.ppermute(x, "head", [(i, i ^ (2, 6)[(i + turn) % 2]) for i in range(count)])


def pair_swap(x):
    count = lax.axis_size("seq")
    return lax.ppermute(x, "seq", [(i, i ^ 1) for i in range(count)])


def one_turn(step, start):
    return lax.fori_loop(0, lax.optimization_barrier(jnp.int32(1)), lambda i, carry: step(), start)


def per_device(
    layer_input, omega_in, upstream, omega_out, q_raw, k_raw, values, d_out, q_gain, k_gain
):
    kv = jnp.concatenate([k_raw, values], axis=1)
    kv, layer_input, upstream = lax.optimization_barrier((kv, layer_input, upstream))
    odd = lax.axis_index("seq") % 2 == 1
    first = lax.axis_index("head") % 2 == 0
    kv2 = shift(kv, 2)
    partial_x = jnp.dot(layer_input, omega_in, preferred_element_type=F32)
    partial_y = jnp.dot(upstream, omega_out, preferred_element_type=F32)
    keep = jnp.where(first, partial_x, partial_y)
    give = jnp.where(first, partial_y, partial_x).astype(BF16)

    def sum_near():
        total = keep + swap(give, 1).astype(F32)
        return (total + z_swap(total.astype(BF16), 0).astype(F32)).astype(BF16)

    half = one_turn(sum_near, keep.astype(BF16))
    kv1 = pair_swap(jnp.where(odd, kv2, kv))
    mine = (half.astype(F32) + z_swap(half, 1).astype(F32)).astype(BF16)
    other = swap(mine, 1)
    x0, y0 = jnp.where(first, mine, other), jnp.where(first, other, mine)
    x1 = shift(x0, 1)
    x2 = shift(x0, 2)
    shard = lax.axis_index("seq").astype(jnp.int32)[None]
    tables = [jnp.asarray(t) for t in rope_tables(lax.axis_size("seq"))]
    query_grad, own, back1, back2, sketches = attention(
        shard, q_raw, d_out, k_raw, values, kv1, kv2, (x0, x1, x2, y0), q_gain, k_gain, tables
    )
    near = pair_swap(back1).astype(F32)
    back2 = back2.astype(F32)
    far = shift(jnp.where(odd, back2 + near, back2).astype(BF16), -2)
    pieces = lax.all_to_all(sketches, "seq", 0, 0, tiled=True)
    total = jnp.sum(pieces.astype(F32), axis=0)
    q_cols, kv_cols = 4 * HD, 2 * HD

    kv_grad = (own.astype(F32) + jnp.where(odd, 0.0, near) + far.astype(F32)).astype(BF16)
    return (
        query_grad,
        kv_grad[:, :kv_cols],
        kv_grad[:, kv_cols:],
        total[:, :q_cols],
        total[:, q_cols : q_cols + kv_cols],
        total[:, q_cols + kv_cols : q_cols + 2 * kv_cols],
        total[:, q_cols + 2 * kv_cols :],
    )


def solution(mesh):
    split = P("seq", "head")
    in_specs = (split, P("head", None), split, P("head", None), split, split, split, split, P(), P())
    return jax.shard_map(
        per_device, mesh=mesh, in_specs=in_specs, out_specs=(split,) * 7, check_vma=False
    )
```
